256 devices in a mesh: band: 16 (over x_hi, y, core), spec: 16 (over z, x_lo).
Axes of the slice: x: 4 (x_hi: 2, x_lo: 2; x = x_hi * 2 + x_lo), y: 4, z: 8, core: 2. Of those that a mesh axis runs over, the one named last changes fastest.
Arguments:
- spectra: float32 [1296, 32, 2048], P(None, 'band', 'spec'), may hold values from 0.05 to 2
- sea_mask: int32 [32, 2048], P('band', 'spec'), may hold values 0 or 1
- wind: float32 [2, 32, 2048], P(None, None, ('spec', 'band')), may hold values from -30 to 30
- current: float32 [2, 32, 2048], P(None, None, ('spec', 'band')), may hold values from -0.2 to 0.2
Outputs:
- spectra_next: float32 [1296, 32, 2048], P(None, 'band', 'spec')
The draws below stay inside these ranges and needn't reach their ends.
All inputs are finite; a program needn't handle non-finite values. No bound on the sum of `sea_mask` on one device may be relied on, other than what follows from the above.
Results may differ from the reference program's by a relative error of at most 0.0003.
Values sent between devices are 32-bit elements; how exact they have to be, the bound alone decides.
A program may use at most 128 MiB of HBM per device.

```python
import math
import jax
import jax.numpy as jnp
from jax import lax

NF = 36
ND = 36
K = 1296
RY = 2
NY = 32
NX = 2048


def place_ends(entries, stream_key, least, high):
    place = [jax.random.randint(jax.random.fold_in(stream_key, axis), (), 0, length) for axis, length in enumerate(entries.shape)]
    widest = entries.shape.index(max(entries.shape))
    neighbour = place[:widest] + [(place[widest] + 1) % entries.shape[widest]] + place[widest + 1:]
    return entries.at[tuple(place)].set(least).at[tuple(neighbour)].set(high)


def shard_levels(rng, shape, pieces, smallest, high):
    loudness, own = 1.0, jax.random.fold_in(rng, 6)
    for dim, parts in pieces:
        heights = jnp.exp(jax.random.uniform(jax.random.fold_in(own, dim), (parts,), jnp.float32, smallest / len(pieces), high / len(pieces)))
        loudness = loudness * jnp.repeat(heights, shape[dim] // parts).reshape([-1 if axis == dim else 1 for axis in range(len(shape))])
    return loudness


def centred(key, dims, spread, most, shards=(), held_as=jnp.bfloat16):
    array = spread * jax.random.normal(key, dims, jnp.float32)
    if shards:
        array = array * shard_levels(key, dims, shards, -0.22, 0.18)
    return jnp.clip(array, -most, most).astype(held_as)


def setup_inputs(seed: int = 0) -> dict:
    streams_of = jax.random.split(jax.random.key(seed), 5)
    spectra = jnp.clip(jnp.exp(math.log(2.0) - 3.6888794 * jax.random.uniform(streams_of[0], (K, NY, NX), jnp.float32) ** shard_levels(streams_of[0], (K, NY, NX), ((1, 16), (2, 16)), -0.2, 0.2)), 0.05, 2.0)
    sea_mask = place_ends((jax.random.randint(streams_of[1], (NY, NX), 0, 10) < 7).astype(jnp.int32), jax.random.fold_in(streams_of[1], 1), 0, 1)
    wind = centred(streams_of[2], (2, NY, NX), 8.0, 30.0, ((2, 256),), jnp.float32)
    current = jnp.clip(jax.random.uniform(streams_of[3], (2, NY, NX), jnp.float32, -0.2, 0.2) * shard_levels(streams_of[3], (2, NY, NX), ((2, 256),), -0.4, 0.0), -0.2, 0.2)
    return dict(spectra=spectra, sea_mask=sea_mask, wind=wind, current=current)


LAT_SOUTH = 30.0
LAT_NORTH = 55.0
SPEED_TOP = 0.35
FREQ_STEP = 1.1
TURNING = 1.5
GROWTH = 0.05
WIND_COUPLING = 0.04


def latitude(position, total_rows):
    return (LAT_SOUTH + (LAT_NORTH - LAT_SOUTH) * position / total_rows) * (math.pi / 180.0)


def wrap_columns(values):
    return jnp.concatenate([values[..., -2:], values, values[..., :2]], axis=-1)


def face_flux(behind, center, ahead, beyond, courant):
    forward = courant >= 0.0
    upwind = jnp.where(forward, behind, beyond)
    source_cell = jnp.where(forward, center, ahead)
    target_cell = jnp.where(forward, ahead, center)
    magnitude = jnp.abs(courant)
    face_value = 0.5 * (source_cell + target_cell) - 0.5 * magnitude * (target_cell - source_cell) - (1.0 - courant * courant) / 6.0 * (target_cell - 2.0 * source_cell + upwind)
    return courant * face_value


def axis_fluxes(extended, cell_courant, along_axis):
    cell_count = extended.shape[along_axis] - 4

    def take_slice(values, offset):
        return lax.slice_in_dim(values, offset, offset + cell_count + 1, axis=along_axis)

    face_courant = 0.5 * (take_slice(cell_courant, 1) + take_slice(cell_courant, 2))
    return face_flux(take_slice(extended, 0), take_slice(extended, 1), take_slice(extended, 2), take_slice(extended, 3), face_courant)


def component_tables(comp_index):
    freq_index = (comp_index // ND).astype(jnp.float32)
    direction = (comp_index % ND).astype(jnp.float32) * (2.0 * math.pi / ND)
    group_speed = SPEED_TOP * jnp.power(jnp.float32(FREQ_STEP), -freq_index)
    return group_speed, jnp.cos(direction), jnp.sin(direction)


def propagate(spec_wide, spec_tall, current_wide, current_tall, comp_index, row_start, total_rows):
    group_speed, cos_dir, sin_dir = component_tables(comp_index)
    row_count = spec_wide.shape[1]
    cell_rows = (row_start + jnp.arange(row_count, dtype=jnp.int32)).astype(jnp.float32) + 0.5
    face_rows = (row_start + jnp.arange(row_count + 1, dtype=jnp.int32)).astype(jnp.float32)
    cell_cos = jnp.cos(latitude(cell_rows, total_rows))
    face_cos = jnp.cos(latitude(face_rows, total_rows))
    east_speed = (group_speed * cos_dir)[:, None, None] / cell_cos[None, :, None] + current_wide[0][None]
    north_speed = (group_speed * sin_dir)[:, None, None] + current_tall[1][None]
    east_flux = axis_fluxes(spec_wide, east_speed, 2)
    north_flux = axis_fluxes(spec_tall, north_speed, 1) * face_cos[None, :, None]
    center_cells = spec_tall[:, 2:-2, :]
    return center_cells - (east_flux[:, :, 1:] - east_flux[:, :, :-1]) - (north_flux[:, 1:, :] - north_flux[:, :-1, :]) / cell_cos[None, :, None]


def point_step(propagated, wind_rows, sea_rows, row_start, total_rows):
    row_count = propagated.shape[2]
    freq_index = jnp.arange(NF, dtype=jnp.int32).astype(jnp.float32)
    direction = jnp.arange(ND, dtype=jnp.int32).astype(jnp.float32) * (2.0 * math.pi / ND)
    group_speed = SPEED_TOP * jnp.power(jnp.float32(FREQ_STEP), -freq_index)
    cell_rows = (row_start + jnp.arange(row_count, dtype=jnp.int32)).astype(jnp.float32) + 0.5
    tangent = jnp.tan(latitude(cell_rows, total_rows))
    turn_rate = -TURNING * group_speed[:, None, None] * jnp.cos(direction)[None, :, None] * tangent[None, None, :]
    turn_wide = jnp.concatenate([turn_rate[:, -2:], turn_rate, turn_rate[:, :2]], axis=1)[..., None]
    spec_wide = jnp.concatenate([propagated[:, -2:], propagated, propagated[:, :2]], axis=1)
    turn_flux = axis_fluxes(spec_wide, turn_wide, 1)
    turned = propagated - (turn_flux[:, 1:] - turn_flux[:, :-1])
    wind_along = wind_rows[0][None] * jnp.cos(direction)[:, None, None] + wind_rows[1][None] * jnp.sin(direction)[:, None, None]
    coupling = WIND_COUPLING * jnp.power(jnp.float32(FREQ_STEP), freq_index)
    growth = GROWTH * jnp.maximum(wind_along[None] * coupling[:, None, None, None] - 1.0, 0.0)
    freq_weight = (freq_index + 1.0) / NF
    steepness = jnp.sum(freq_weight[:, None, None, None] * turned * turned, axis=(0, 1)) * (2.0 / (NF * ND))
    damping = 1.0 + freq_weight[:, None, None, None] * steepness[None, None]
    return sea_rows[None, None] * turned * (1.0 + growth) / damping


def reference(spectra, sea_mask, wind, current):
    comp_count, total_rows, total_cols = spectra.shape
    sea_float = sea_mask.astype(jnp.float32)
    current_wide = wrap_columns(current)
    current_tall = jnp.pad(current, ((0, 0), (2, 2), (0, 0)))

    def prop_block(freq_step, done):
        start_comp = (freq_step * ND).astype(jnp.int32)
        block_spec = lax.dynamic_slice_in_dim(spectra, start_comp, ND, 0) * sea_float[None]
        comp_index = start_comp + jnp.arange(ND, dtype=jnp.int32)
        spec_wide = wrap_columns(block_spec)
        spec_tall = jnp.pad(block_spec, ((0, 0), (2, 2), (0, 0)))
        result = propagate(spec_wide, spec_tall, current_wide, current_tall, comp_index, 0, total_rows)
        return lax.dynamic_update_slice_in_dim(done, result, start_comp, 0)

    propagated = lax.fori_loop(0, NF, prop_block, jnp.zeros_like(spectra))

    def point_block(row_step, done):
        start_row = (row_step * RY).astype(jnp.int32)
        piece_spec = lax.dynamic_slice_in_dim(propagated, start_row, RY, 1).reshape(NF, ND, RY, total_cols)
        wind_rows = lax.dynamic_slice_in_dim(wind, start_row, RY, 1)
        sea_rows = lax.dynamic_slice_in_dim(sea_float, start_row, RY, 0)
        result = point_step(piece_spec, wind_rows, sea_rows, start_row, total_rows).reshape(comp_count, RY, total_cols)
        return lax.dynamic_update_slice_in_dim(done, result, start_row, 1)

    return lax.fori_loop(0, total_rows // RY, point_block, jnp.zeros_like(spectra))
```

```python
import functools
import math

import jax
import jax.numpy as jnp
import numpy as np
from jax import lax
from jax.experimental import pallas as pl
from jax.experimental.pallas import tpu as pltpu
from jax.sharding import PartitionSpec as P

NF = 36
ND = 36

LAT_SOUTH = 30.0
LAT_NORTH = 55.0
SPEED_TOP = 0.35
FREQ_STEP = 1.1
TURNING = 1.5
GROWTH = 0.05
WIND_COUPLING = 0.04

MESH = pl.DeviceIdType.MESH
LANES = 128
ROWS = 2
VPF = ND * ROWS // 8
FPG = 3
GROUPS = NF // FPG
GROUP_ROWS = FPG * ND * ROWS
ROWS_ALL = NF * ND * ROWS


def tables(bands):
    total = bands * ROWS
    rad = math.pi / 180.0

    def lat(p):
        return (LAT_SOUTH + (LAT_NORTH - LAT_SOUTH) * p / total) * rad

    geo = np.zeros((bands, 8), np.float64)
    for b in range(bands):
        y = b * ROWS
        c0, c1 = math.cos(lat(y + 0.5)), math.cos(lat(y + 1.5))
        fs, fm, fn = math.cos(lat(y)), math.cos(lat(y + 1)), math.cos(lat(y + 2))
        geo[b] = [
            1.0 / c0, 1.0 / c1,
            0.5 * fs / c0, 0.5 * fm / c1,
            0.5 * fm / c0, 0.5 * fn / c1,
            math.tan(lat(y + 0.5)), math.tan(lat(y + 1.5)),
        ]
    f = np.arange(NF)
    speed = SPEED_TOP * FREQ_STEP ** (-f)
    wave = np.stack([speed, GROWTH * WIND_COUPLING * FREQ_STEP**f, (f + 1.0) / NF], 1)
    theta = 2.0 * math.pi * np.arange(ND) / ND
    cos, sin = np.cos(theta), np.sin(theta)
    turn = -TURNING * 0.5 * (np.roll(cos, 1) + cos)

    def spread(v):
        return np.broadcast_to(np.repeat(v, ROWS)[:, None], (ND * ROWS, LANES))

    trig = np.stack([spread(cos), spread(sin), spread(turn)]).astype(np.float32)
    return geo.astype(np.float32).reshape(-1), wave.astype(np.float32).reshape(-1), trig


def face(c, low, high, step, bend_low, bend_high):
    bend = jnp.where(c >= 0.0, bend_low, bend_high)
    return c * (((low + high) - c * step) + (c * c * (1.0 / 3.0) - 1.0 / 3.0) * bend)


def two_faces(c_low, c_high, low2, low, mid, high, high2):
    d0, d1, d2, d3 = low - low2, mid - low, high - mid, high2 - high
    k0, k1, k2 = d1 - d0, d2 - d1, d3 - d2
    return face(c_low, low, mid, d1, k0, k1), face(c_high, mid, high, d2, k1, k2)


def kernel(
    bands, specs,
    geo, wave, x_hbm, mask_ref, wind_ref, cur_ref, trig_ref,
    av, damp_ref,
    xv, south, north, mask_s, mask_n, square, strip, out_msg, in_msg, in_west, in_east,
    pack, pack_w, pack_e, cct, tnt, wnd, pbuf, fbuf,
    x_sem, msg_send, msg_recv, edge_send, edge_recv, pack_send, pack_recv, mask_send, mask_recv,
    n_send, s_send, n_recv, s_recv,
):
    b = lax.axis_index("band")
    s = lax.axis_index("spec")
    west, east = lax.rem(s + specs - 1, specs), lax.rem(s + 1, specs)
    has_n, has_s = b < bands - 1, b > 0
    up_band, down_band = jnp.minimum(b + 1, bands - 1), jnp.maximum(b - 1, 0)
    cols = LANES // bands

    barrier = pltpu.get_barrier_semaphore()
    for d in range(1, bands):
        pl.semaphore_signal(barrier, inc=1, device_id=(lax.rem(b + d, bands), s), device_id_type=MESH)
    for target in ((b, west), (b, east)):
        pl.semaphore_signal(barrier, inc=1, device_id=target, device_id_type=MESH)

    @pl.when(b < bands - 1)
    def _():
        pl.semaphore_signal(barrier, inc=1, device_id=(bands - 1, west), device_id_type=MESH)

    @pl.when(b > 0)
    def _():
        pl.semaphore_signal(barrier, inc=1, device_id=(0, east), device_id_type=MESH)

    load = pltpu.make_async_copy(x_hbm, xv, x_sem)
    load.start()

    sub = lax.broadcasted_iota(jnp.int32, (8, LANES), 0)
    lane = lax.broadcasted_iota(jnp.int32, (8, LANES), 1)
    even = lax.rem(sub, 2) == 0

    def pair(a, c):
        return jnp.where(even, a, c)

    square[...] = jnp.zeros_like(square)
    for i in range(2):
        square[i * 8 : i * 8 + cols, 0 : bands * ROWS] = wind_ref[i]
        square[16 + i * 8 : 16 + i * 8 + cols, 0 : bands * ROWS] = cur_ref[i]
    strip[...] = jnp.zeros_like(strip)
    strip[8 : 8 + bands * ROWS, :] = square[...].T[0 : bands * ROWS, :]
    message = strip[pl.ds(8, bands, stride=2), :]
    for q, first in ((1, 9), (2, 7), (3, 10)):
        message = message + pltpu.roll(strip[pl.ds(first, bands, stride=2), :], 32 * q, 1)
    for d in range(bands):
        out_msg[d] = message[d : d + 1]

    sea = mask_ref[...].astype(jnp.float32)
    sea_t = pair(sea[0:1], sea[1:2])

    load.wait()

    def pack_group(g, carry):
        acc = jnp.zeros((8, LANES), jnp.float32)
        for i in range(FPG * VPF):
            v = xv[pl.ds(pl.multiple_of(g * GROUP_ROWS + 8 * i, 8), 8), :] * sea_t
            acc = jnp.where((lane >= 4 * i) & (lane < 4 * i + 4), pltpu.roll(v, 4 * i + 2, 1), acc)
        pack[pl.ds(pl.multiple_of(g * 8, 8), 8), :] = acc
        return carry

    lax.fori_loop(0, GROUPS, pack_group, 0)

    at_end = (b == 0) | (b == bands - 1)

    @pl.when(at_end)
    def _():
        pl.semaphore_wait(barrier, 2 * bands)

    @pl.when(jnp.logical_not(at_end))
    def _():
        pl.semaphore_wait(barrier, bands + 1)

    def msg_copy(d, source):
        target = lax.rem(b + d, bands)
        return pltpu.make_async_remote_copy(
            src_ref=out_msg.at[target], dst_ref=in_msg.at[source], send_sem=msg_send.at[d], recv_sem=msg_recv.at[d],
            device_id=(target, s), device_id_type=MESH,
        )

    for d in range(1, bands):
        msg_copy(d, b).start()

    def edge_copy(t, to_east):
        return pltpu.make_async_remote_copy(
            src_ref=out_msg.at[t], dst_ref=in_west if to_east else in_east,
            send_sem=edge_send.at[t], recv_sem=edge_recv.at[0 if to_east else 1],
            device_id=(t, east if to_east else west), device_id_type=MESH,
        )

    @pl.when(b == bands - 1)
    def _():
        for t in range(bands):
            edge_copy(t, True).start()

    @pl.when(b == 0)
    def _():
        for t in range(bands):
            edge_copy(t, False).start()

    def chunk(g):
        return pl.ds(pl.multiple_of(g * GROUP_ROWS, GROUP_ROWS), GROUP_ROWS)

    def to_north(g):
        return pltpu.make_async_remote_copy(
            src_ref=x_hbm.at[chunk(g)], dst_ref=south.at[chunk(g)], send_sem=n_send.at[g], recv_sem=s_recv.at[g],
            device_id=(up_band, s), device_id_type=MESH,
        )

    def to_south(g):
        return pltpu.make_async_remote_copy(
            src_ref=x_hbm.at[chunk(g)], dst_ref=north.at[chunk(g)], send_sem=s_send.at[g], recv_sem=n_recv.at[g],
            device_id=(down_band, s), device_id_type=MESH,
        )

    def mask_copy(northward):
        return pltpu.make_async_remote_copy(
            src_ref=mask_ref, dst_ref=mask_s if northward else mask_n,
            send_sem=mask_send.at[0 if northward else 1], recv_sem=mask_recv.at[0 if northward else 1],
            device_id=(up_band if northward else down_band, s), device_id_type=MESH,
        )

    def pack_copy(to_east):
        return pltpu.make_async_remote_copy(
            src_ref=pack, dst_ref=pack_w if to_east else pack_e,
            send_sem=pack_send.at[0 if to_east else 1], recv_sem=pack_recv.at[0 if to_east else 1],
            device_id=(b, east if to_east else west), device_id_type=MESH,
        )

    @pl.when(has_n)
    def _():
        mask_copy(True).start()

    @pl.when(has_s)
    def _():
        mask_copy(False).start()

    pack_copy(True).start()
    pack_copy(False).start()

    def send_chunk(g, carry):
        @pl.when(has_n)
        def _():
            to_north(g).start()

        @pl.when(has_s)
        def _():
            to_south(g).start()

        return carry

    lax.fori_loop(0, GROUPS, send_chunk, 0)

    @pl.when(b == 0)
    def _():
        mask_s[...] = jnp.zeros_like(mask_s)

        def clear(i, carry):
            south[pl.ds(pl.multiple_of(i * GROUP_ROWS, 8), GROUP_ROWS), :] = jnp.zeros((GROUP_ROWS, LANES), jnp.float32)
            return carry

        lax.fori_loop(0, GROUPS, clear, 0)

    @pl.when(b == bands - 1)
    def _():
        mask_n[...] = jnp.zeros_like(mask_n)

        def clear(i, carry):
            north[pl.ds(pl.multiple_of(i * GROUP_ROWS, 8), GROUP_ROWS), :] = jnp.zeros((GROUP_ROWS, LANES), jnp.float32)
            return carry

        lax.fori_loop(0, GROUPS, clear, 0)

    g0 = b * 8
    inv_cos = pair(geo[g0], geo[g0 + 1])
    metric_a = pair(geo[g0 + 2], geo[g0 + 3])
    metric_b = pair(geo[g0 + 4], geo[g0 + 5])
    tangent = pair(geo[g0 + 6], geo[g0 + 7])
    for j in range(VPF):
        at = slice(8 * j, 8 * j + 8)
        cct[at, :] = trig_ref[0, at, :] * inv_cos
        tnt[at, :] = trig_ref[2, at, :] * tangent

    in_msg[b] = out_msg[b]
    for d in range(1, bands):
        msg_copy(d, lax.rem(b + bands - d, bands)).wait_recv()
    edge_copy(0, True).wait_recv()
    edge_copy(0, False).wait_recv()

    got = jnp.concatenate(
        [
            pltpu.roll(jnp.concatenate([in_msg[h + d] for d in range(8)], axis=0), h * cols, 1, stride=cols, stride_axis=0)
            for h in range(0, bands, 8)
        ],
        axis=0,
    )
    own = lax.broadcasted_iota(jnp.int32, (bands, LANES), 1) // cols == lax.broadcasted_iota(jnp.int32, (bands, LANES), 0)

    def field(q, f):
        moved = pltpu.roll(got, (LANES - 32 * q - 8 * f) % LANES, 1)
        return jnp.sum(jnp.where(own, moved, 0.0), axis=0, keepdims=True)

    w0 = pair(field(0, 0), field(1, 0))
    w1 = pair(field(0, 1), field(1, 1))
    u = pair(field(0, 2), field(1, 2))
    v0, v1, vs, vn = field(0, 3), field(1, 3), field(2, 3), field(3, 3)
    wm = jnp.broadcast_to(in_west[...], (8, LANES))
    em = jnp.broadcast_to(in_east[...], (8, LANES))
    u_w = pair(pltpu.roll(wm, LANES - 1 - (16 + cols - 1), 1), pltpu.roll(wm, LANES - 1 - (48 + cols - 1), 1))
    u_e = pair(pltpu.roll(em, LANES - 16, 1), pltpu.roll(em, LANES - 48, 1))
    c_west = 0.5 * (u + pltpu.roll(jnp.where(lane == LANES - 1, u_w, u), 1, 1))
    c_east = 0.5 * (u + pltpu.roll(jnp.where(lane == 0, u_e, u), LANES - 1, 1))
    c_south = 0.5 * pair(vs + v0, v0 + v1)
    c_north = 0.5 * pair(v0 + v1, v1 + vn)
    for j in range(VPF):
        at = slice(8 * j, 8 * j + 8)
        wnd[at, :] = w0 * trig_ref[0, at, :] + w1 * trig_ref[1, at, :]

    pack_copy(True).wait_recv()
    pack_copy(False).wait_recv()

    @pl.when(has_s)
    def _():
        mask_copy(True).wait_recv()

    @pl.when(has_n)
    def _():
        mask_copy(False).wait_recv()

    ms, mn = mask_s[...].astype(jnp.float32), mask_n[...].astype(jnp.float32)
    sea_s = pair(ms[0:1], ms[1:2])
    sea_n = pair(mn[0:1], mn[1:2])
    from_west = lax.rem(lane, 4) < 2

    def group(g, total):
        @pl.when(has_s)
        def _():
            to_north(g).wait_recv()

        @pl.when(has_n)
        def _():
            to_south(g).wait_recv()

        prow = pl.ds(pl.multiple_of(g * 8, 8), 8)
        beside = jnp.where(from_west, pack_w[prow, :], pack_e[prow, :])
        for k in range(FPG):
            f = g * FPG + k
            speed, growth, weight = wave[3 * f], wave[3 * f + 1], wave[3 * f + 2]
            base = g * GROUP_ROWS + k * ND * ROWS
            for j in range(VPF):
                at = slice(8 * j, 8 * j + 8)
                rows = pl.ds(pl.multiple_of(base + 8 * j, 8), 8)
                x = xv[rows, :] * sea_t
                halo = pltpu.roll(beside, LANES - (4 * (k * VPF + j) + 2), 1)
                w1, w2 = jnp.where(lane == LANES - 1, halo, x), jnp.where(lane >= LANES - 2, halo, x)
                e1, e2 = jnp.where(lane == 0, halo, x), jnp.where(lane < 2, halo, x)
                c = speed * cct[at, :]
                fw, fe = two_faces(
                    c + c_west, c + c_east,
                    pltpu.roll(w2, 2, 1), pltpu.roll(w1, 1, 1), x, pltpu.roll(e1, LANES - 1, 1), pltpu.roll(e2, LANES - 2, 1),
                )
                xs = south[rows, :] * sea_s
                xn = north[rows, :] * sea_n
                below = pair(pltpu.roll(xs, 7, 0), pltpu.roll(x, 1, 0))
                above = pair(pltpu.roll(x, 7, 0), pltpu.roll(xn, 1, 0))
                c = speed * trig_ref[1, at, :]
                fs, fn = two_faces(c + c_south, c + c_north, xs, below, x, above, xn)
                out = x - 0.5 * (fe - fw) - (metric_b * fn - metric_a * fs)
                pbuf[k, 8 + 8 * j : 16 + 8 * j, :] = out
                if j == 0:
                    pbuf[k, 8 + ND * ROWS : 16 + ND * ROWS, :] = out
                if j == VPF - 1:
                    pbuf[k, 0:8, :] = out
            for j in range(VPF):
                at = slice(8 * j, 8 * j + 8)
                o = 8 + 8 * j
                low2, low, mid, high = (pbuf[k, o + i : o + i + 8, :] for i in (-4, -2, 0, 2))
                d0, d1, d2 = low - low2, mid - low, high - mid
                flux = face(speed * tnt[at, :], low, mid, d1, d1 - d0, d2 - d1)
                fbuf[k, at, :] = flux
                if j == 0:
                    fbuf[k, ND * ROWS : ND * ROWS + 8, :] = flux
            square_sum = jnp.zeros((8, LANES), jnp.float32)
            for j in range(VPF):
                at = slice(8 * j, 8 * j + 8)
                rows = pl.ds(pl.multiple_of(base + 8 * j, 8), 8)
                turned = pbuf[k, 8 + 8 * j : 16 + 8 * j, :] - 0.5 * (fbuf[k, 8 * j + 2 : 8 * j + 10, :] - fbuf[k, at, :])
                square_sum = square_sum + turned * turned
                av[rows, :] = (sea_t * turned) * jnp.maximum(growth * wnd[at, :] + (1.0 - GROWTH), 1.0)
            total = total + weight * square_sum
        return total

    total = lax.fori_loop(0, GROUPS, group, jnp.zeros((8, LANES), jnp.float32))
    total = total + pltpu.roll(total, 4, 0)
    total = (total + pltpu.roll(total, 2, 0)) * (2.0 / (NF * ND))
    for f in range(NF):
        damp_ref[f] = 1.0 / (1.0 + total * ((f + 1.0) / NF))

    def finish(g, carry):
        @pl.when(has_n)
        def _():
            to_north(g).wait_send()

        @pl.when(has_s)
        def _():
            to_south(g).wait_send()

        return carry

    lax.fori_loop(0, GROUPS, finish, 0)
    for d in range(1, bands):
        msg_copy(d, b).wait_send()

    @pl.when(b == bands - 1)
    def _():
        for t in range(bands):
            edge_copy(t, True).wait_send()

    @pl.when(b == 0)
    def _():
        for t in range(bands):
            edge_copy(t, False).wait_send()

    pack_copy(True).wait_send()
    pack_copy(False).wait_send()

    @pl.when(has_n)
    def _():
        mask_copy(True).wait_send()

    @pl.when(has_s)
    def _():
        mask_copy(False).wait_send()


def damped(a_ref, damp_ref, o_hbm, ov, sem):
    for g in range(GROUPS):
        at = pl.ds(g * GROUP_ROWS, GROUP_ROWS)
        for k in range(FPG):
            factor = damp_ref[g * FPG + k]
            for j in range(VPF):
                rows = slice(g * GROUP_ROWS + 8 * (k * VPF + j), g * GROUP_ROWS + 8 * (k * VPF + j) + 8)
                ov[rows, :] = a_ref[rows, :] * factor
        pltpu.make_async_copy(ov.at[at], o_hbm.at[at], sem.at[g]).start()
    for g in range(GROUPS):
        at = pl.ds(g * GROUP_ROWS, GROUP_ROWS)
        pltpu.make_async_copy(ov.at[at], o_hbm.at[at], sem.at[g]).wait()


def per_device(bands, specs, spectra, sea_mask, wind, current):
    rows_all = ROWS_ALL
    geo, wave, trig = tables(bands)
    f32 = jnp.float32
    vmem = pl.BlockSpec(memory_space=pltpu.VMEM)
    smem = pl.BlockSpec(memory_space=pltpu.SMEM)
    hbm = pl.BlockSpec(memory_space=pl.ANY)
    dma = pltpu.SemaphoreType.DMA
    grown, damp = pl.pallas_call(
        functools.partial(kernel, bands, specs),
        out_shape=(
            pltpu.VMEM((rows_all, LANES), f32),
            pltpu.VMEM((NF, 8, LANES), f32),
        ),
        in_specs=[smem, smem, hbm, vmem, vmem, vmem, vmem],
        out_specs=(vmem, vmem),
        scratch_shapes=[
            pltpu.VMEM((rows_all, LANES), f32),
            pltpu.VMEM((rows_all, LANES), f32),
            pltpu.VMEM((rows_all, LANES), f32),
            pltpu.VMEM((ROWS, LANES), jnp.int32),
            pltpu.VMEM((ROWS, LANES), jnp.int32),
            pltpu.VMEM((LANES, LANES), f32),
            pltpu.VMEM((48, LANES), f32),
            pltpu.VMEM((bands, 1, LANES), f32),
            pltpu.VMEM((bands, 1, LANES), f32),
            pltpu.VMEM((1, LANES), f32),
            pltpu.VMEM((1, LANES), f32),
            pltpu.VMEM((GROUPS * 8, LANES), f32),
            pltpu.VMEM((GROUPS * 8, LANES), f32),
            pltpu.VMEM((GROUPS * 8, LANES), f32),
            pltpu.VMEM((ND * ROWS, LANES), f32),
            pltpu.VMEM((ND * ROWS, LANES), f32),
            pltpu.VMEM((ND * ROWS, LANES), f32),
            pltpu.VMEM((FPG, ND * ROWS + 16, LANES), f32),
            pltpu.VMEM((FPG, ND * ROWS + 8, LANES), f32),
            dma(()), dma((bands,)), dma((bands,)), dma((bands,)), dma((2,)),
            dma((2,)), dma((2,)), dma((2,)), dma((2,)),
            dma((GROUPS,)), dma((GROUPS,)), dma((GROUPS,)), dma((GROUPS,)),
        ],
        compiler_params=pltpu.CompilerParams(collective_id=0, has_side_effects=True),
        name="wave_step",
    )(
        jnp.asarray(geo), jnp.asarray(wave),
        spectra.reshape(rows_all, LANES), sea_mask,
        wind.transpose(0, 2, 1), current.transpose(0, 2, 1), jnp.asarray(trig),
    )
    out = pl.pallas_call(
        damped,
        out_shape=jax.ShapeDtypeStruct((rows_all, LANES), f32),
        in_specs=[vmem, vmem],
        out_specs=hbm,
        scratch_shapes=[pltpu.VMEM((rows_all, LANES), f32), dma((GROUPS,))],
        name="damped",
    )(*(pltpu.with_memory_space_constraint(v, pltpu.VMEM) for v in (grown, damp)))
    return out.reshape(NF * ND, ROWS, LANES)


def solution(mesh):
    placed = (
        P(None, "band", "spec"),
        P("band", "spec"),
        P(None, None, ("spec", "band")),
        P(None, None, ("spec", "band")),
    )
    return jax.shard_map(
        functools.partial(per_device, mesh.shape["band"], mesh.shape["spec"]),
        mesh=mesh, in_specs=placed, out_specs=P(None, "band", "spec"), check_vma=False,
    )
```

```python
import functools
import math

import jax
import jax.numpy as jnp
import numpy as np
from jax import lax
from jax.experimental import pallas as pl
from jax.experimental.pallas import tpu as pltpu
from jax.sharding import PartitionSpec as P

NF = 36
ND = 36

LAT_SOUTH = 30.0
LAT_NORTH = 55.0
SPEED_TOP = 0.35
FREQ_STEP = 1.1
TURNING = 1.5
GROWTH = 0.05
WIND_COUPLING = 0.04

MESH = pl.DeviceIdType.MESH
LANES = 128
ROWS = 2
VPF = ND * ROWS // 8
FPG = 3
GROUPS = NF // FPG
GROUP_ROWS = FPG * ND * ROWS
ROWS_ALL = NF * ND * ROWS


def tables(bands):
    total = bands * ROWS
    rad = math.pi / 180.0

    def lat(p):
        return (LAT_SOUTH + (LAT_NORTH - LAT_SOUTH) * p / total) * rad

    geo = np.zeros((bands, 8), np.float64)
    for b in range(bands):
        y = b * ROWS
        c0, c1 = math.cos(lat(y + 0.5)), math.cos(lat(y + 1.5))
        fs, fm, fn = math.cos(lat(y)), math.cos(lat(y + 1)), math.cos(lat(y + 2))
        geo[b] = [
            1.0 / c0, 1.0 / c1,
            0.5 * fs / c0, 0.5 * fm / c1,
            0.5 * fm / c0, 0.5 * fn / c1,
            math.tan(lat(y + 0.5)), math.tan(lat(y + 1.5)),
        ]
    f = np.arange(NF)
    speed = SPEED_TOP * FREQ_STEP ** (-f)
    wave = np.stack([speed, GROWTH * WIND_COUPLING * FREQ_STEP**f, (f + 1.0) / NF], 1)
    theta = 2.0 * math.pi * np.arange(ND) / ND
    cos, sin = np.cos(theta), np.sin(theta)
    turn = -TURNING * 0.5 * (np.roll(cos, 1) + cos)

    def spread(v):
        return np.broadcast_to(np.repeat(v, ROWS)[:, None], (ND * ROWS, LANES))

    trig = np.stack([spread(cos), spread(sin), spread(turn)]).astype(np.float32)
    return geo.astype(np.float32).reshape(-1), wave.astype(np.float32).reshape(-1), trig


def face(c, low, high, step, bend_low, bend_high):
    bend = jnp.where(c >= 0.0, bend_low, bend_high)
    return c * (((low + high) - c * step) + (c * c * (1.0 / 3.0) - 1.0 / 3.0) * bend)


def two_faces(c_low, c_high, low2, low, mid, high, high2):
    d0, d1, d2, d3 = low - low2, mid - low, high - mid, high2 - high
    k0, k1, k2 = d1 - d0, d2 - d1, d3 - d2
    return face(c_low, low, mid, d1, k0, k1), face(c_high, mid, high, d2, k1, k2)


def kernel(
    bands, specs,
    geo_hbm, wave_hbm, x_hbm, mask_hbm, wind_hbm, cur_hbm, trig_hbm,
    av, damp_ref,
    geo, wave, mask_ref, wind_ref, cur_ref, trig_ref, small_sem,
    xv, south, north, mask_s, mask_n, square, strip, out_msg, in_msg, in_west, in_east,
    pack, pack_w, pack_e, cct, tnt, wnd, pbuf, fbuf,
    x_sem, msg_send, msg_recv, edge_send, edge_recv, pack_send, pack_recv, mask_send, mask_recv,
    n_send, s_send, n_recv, s_recv,
):
    b = lax.axis_index("band")
    s = lax.axis_index("spec")
    west, east = lax.rem(s + specs - 1, specs), lax.rem(s + 1, specs)
    has_n, has_s = b < bands - 1, b > 0
    up_band, down_band = jnp.minimum(b + 1, bands - 1), jnp.maximum(b - 1, 0)
    cols = LANES // bands

    barrier = pltpu.get_barrier_semaphore()
    for d in range(1, bands):
        pl.semaphore_signal(barrier, inc=1, device_id=(lax.rem(b + d, bands), s), device_id_type=MESH)
    for target in ((b, west), (b, east)):
        pl.semaphore_signal(barrier, inc=1, device_id=target, device_id_type=MESH)

    @pl.when(b < bands - 1)
    def _():
        pl.semaphore_signal(barrier, inc=1, device_id=(bands - 1, west), device_id_type=MESH)

    @pl.when(b > 0)
    def _():
        pl.semaphore_signal(barrier, inc=1, device_id=(0, east), device_id_type=MESH)

    small = [
        pltpu.make_async_copy(a, v, small_sem.at[i])
        for i, (a, v) in enumerate((
            (wind_hbm, wind_ref), (cur_hbm, cur_ref), (mask_hbm, mask_ref),
            (geo_hbm, geo), (wave_hbm, wave), (trig_hbm, trig_ref),
        ))
    ]
    for copy in small[:3]:
        copy.start()
    load = pltpu.make_async_copy(x_hbm, xv, x_sem)
    load.start()
    for copy in small[3:]:
        copy.start()

    sub = lax.broadcasted_iota(jnp.int32, (8, LANES), 0)
    lane = lax.broadcasted_iota(jnp.int32, (8, LANES), 1)
    even = lax.rem(sub, 2) == 0

    def pair(a, c):
        return jnp.where(even, a, c)

    square[...] = jnp.zeros_like(square)
    for copy in small[:3]:
        copy.wait()
    for i in range(2):
        square[i * 8 : i * 8 + cols, 0 : bands * ROWS] = wind_ref[i]
        square[16 + i * 8 : 16 + i * 8 + cols, 0 : bands * ROWS] = cur_ref[i]
    strip[...] = jnp.zeros_like(strip)
    strip[8 : 8 + bands * ROWS, :] = square[...].T[0 : bands * ROWS, :]
    message = strip[pl.ds(8, bands, stride=2), :]
    for q, first in ((1, 9), (2, 7), (3, 10)):
        message = message + pltpu.roll(strip[pl.ds(first, bands, stride=2), :], 32 * q, 1)
    for d in range(bands):
        out_msg[d] = message[d : d + 1]

    sea = mask_ref[...].astype(jnp.float32)
    sea_t = pair(sea[0:1], sea[1:2])

    load.wait()

    def pack_group(g, carry):
        acc = jnp.zeros((8, LANES), jnp.float32)
        for i in range(FPG * VPF):
            v = xv[pl.ds(pl.multiple_of(g * GROUP_ROWS + 8 * i, 8), 8), :] * sea_t
            acc = jnp.where((lane >= 4 * i) & (lane < 4 * i + 4), pltpu.roll(v, 4 * i + 2, 1), acc)
        pack[pl.ds(pl.multiple_of(g * 8, 8), 8), :] = acc
        return carry

    lax.fori_loop(0, GROUPS, pack_group, 0)

    at_end = (b == 0) | (b == bands - 1)

    @pl.when(at_end)
    def _():
        pl.semaphore_wait(barrier, 2 * bands)

    @pl.when(jnp.logical_not(at_end))
    def _():
        pl.semaphore_wait(barrier, bands + 1)

    def msg_copy(d, source):
        target = lax.rem(b + d, bands)
        return pltpu.make_async_remote_copy(
            src_ref=out_msg.at[target], dst_ref=in_msg.at[source], send_sem=msg_send.at[d], recv_sem=msg_recv.at[d],
            device_id=(target, s), device_id_type=MESH,
        )

    for d in range(1, bands):
        msg_copy(d, b).start()

    def edge_copy(t, to_east):
        return pltpu.make_async_remote_copy(
            src_ref=out_msg.at[t], dst_ref=in_west if to_east else in_east,
            send_sem=edge_send.at[t], recv_sem=edge_recv.at[0 if to_east else 1],
            device_id=(t, east if to_east else west), device_id_type=MESH,
        )

    @pl.when(b == bands - 1)
    def _():
        for t in range(bands):
            edge_copy(t, True).start()

    @pl.when(b == 0)
    def _():
        for t in range(bands):
            edge_copy(t, False).start()

    def chunk(g):
        return pl.ds(pl.multiple_of(g * GROUP_ROWS, GROUP_ROWS), GROUP_ROWS)

    def to_north(g):
        return pltpu.make_async_remote_copy(
            src_ref=x_hbm.at[chunk(g)], dst_ref=south.at[chunk(g)], send_sem=n_send.at[g], recv_sem=s_recv.at[g],
            device_id=(up_band, s), device_id_type=MESH,
        )

    def to_south(g):
        return pltpu.make_async_remote_copy(
            src_ref=x_hbm.at[chunk(g)], dst_ref=north.at[chunk(g)], send_sem=s_send.at[g], recv_sem=n_recv.at[g],
            device_id=(down_band, s), device_id_type=MESH,
        )

    def mask_copy(northward):
        return pltpu.make_async_remote_copy(
            src_ref=mask_ref, dst_ref=mask_s if northward else mask_n,
            send_sem=mask_send.at[0 if northward else 1], recv_sem=mask_recv.at[0 if northward else 1],
            device_id=(up_band if northward else down_band, s), device_id_type=MESH,
        )

    def pack_copy(to_east):
        return pltpu.make_async_remote_copy(
            src_ref=pack, dst_ref=pack_w if to_east else pack_e,
            send_sem=pack_send.at[0 if to_east else 1], recv_sem=pack_recv.at[0 if to_east else 1],
            device_id=(b, east if to_east else west), device_id_type=MESH,
        )

    @pl.when(has_n)
    def _():
        mask_copy(True).start()

    @pl.when(has_s)
    def _():
        mask_copy(False).start()

    pack_copy(True).start()
    pack_copy(False).start()

    def send_chunk(g, carry):
        @pl.when(has_n)
        def _():
            to_north(g).start()

        @pl.when(has_s)
        def _():
            to_south(g).start()

        return carry

    lax.fori_loop(0, GROUPS, send_chunk, 0)

    @pl.when(b == 0)
    def _():
        mask_s[...] = jnp.zeros_like(mask_s)

        def clear(i, carry):
            south[pl.ds(pl.multiple_of(i * GROUP_ROWS, 8), GROUP_ROWS), :] = jnp.zeros((GROUP_ROWS, LANES), jnp.float32)
            return carry

        lax.fori_loop(0, GROUPS, clear, 0)

    @pl.when(b == bands - 1)
    def _():
        mask_n[...] = jnp.zeros_like(mask_n)

        def clear(i, carry):
            north[pl.ds(pl.multiple_of(i * GROUP_ROWS, 8), GROUP_ROWS), :] = jnp.zeros((GROUP_ROWS, LANES), jnp.float32)
            return carry

        lax.fori_loop(0, GROUPS, clear, 0)

    for copy in small[3:]:
        copy.wait()
    g0 = b * 8
    inv_cos = pair(geo[g0], geo[g0 + 1])
    metric_a = pair(geo[g0 + 2], geo[g0 + 3])
    metric_b = pair(geo[g0 + 4], geo[g0 + 5])
    tangent = pair(geo[g0 + 6], geo[g0 + 7])
    for j in range(VPF):
        at = slice(8 * j, 8 * j + 8)
        cct[at, :] = trig_ref[0, at, :] * inv_cos
        tnt[at, :] = trig_ref[2, at, :] * tangent

    in_msg[b] = out_msg[b]
    for d in range(1, bands):
        msg_copy(d, lax.rem(b + bands - d, bands)).wait_recv()
    edge_copy(0, True).wait_recv()
    edge_copy(0, False).wait_recv()

    got = jnp.concatenate(
        [
            pltpu.roll(jnp.concatenate([in_msg[h + d] for d in range(8)], axis=0), h * cols, 1, stride=cols, stride_axis=0)
            for h in range(0, bands, 8)
        ],
        axis=0,
    )
    own = lax.broadcasted_iota(jnp.int32, (bands, LANES), 1) // cols == lax.broadcasted_iota(jnp.int32, (bands, LANES), 0)

    def field(q, f):
        moved = pltpu.roll(got, (LANES - 32 * q - 8 * f) % LANES, 1)
        return jnp.sum(jnp.where(own, moved, 0.0), axis=0, keepdims=True)

    w0 = pair(field(0, 0), field(1, 0))
    w1 = pair(field(0, 1), field(1, 1))
    u = pair(field(0, 2), field(1, 2))
    v0, v1, vs, vn = field(0, 3), field(1, 3), field(2, 3), field(3, 3)
    wm = jnp.broadcast_to(in_west[...], (8, LANES))
    em = jnp.broadcast_to(in_east[...], (8, LANES))
    u_w = pair(pltpu.roll(wm, LANES - 1 - (16 + cols - 1), 1), pltpu.roll(wm, LANES - 1 - (48 + cols - 1), 1))
    u_e = pair(pltpu.roll(em, LANES - 16, 1), pltpu.roll(em, LANES - 48, 1))
    c_west = 0.5 * (u + pltpu.roll(jnp.where(lane == LANES - 1, u_w, u), 1, 1))
    c_east = 0.5 * (u + pltpu.roll(jnp.where(lane == 0, u_e, u), LANES - 1, 1))
    c_south = 0.5 * pair(vs + v0, v0 + v1)
    c_north = 0.5 * pair(v0 + v1, v1 + vn)
    for j in range(VPF):
        at = slice(8 * j, 8 * j + 8)
        wnd[at, :] = w0 * trig_ref[0, at, :] + w1 * trig_ref[1, at, :]

    pack_copy(True).wait_recv()
    pack_copy(False).wait_recv()

    @pl.when(has_s)
    def _():
        mask_copy(True).wait_recv()

    @pl.when(has_n)
    def _():
        mask_copy(False).wait_recv()

    ms, mn = mask_s[...].astype(jnp.float32), mask_n[...].astype(jnp.float32)
    sea_s = pair(ms[0:1], ms[1:2])
    sea_n = pair(mn[0:1], mn[1:2])
    from_west = lax.rem(lane, 4) < 2

    def group(g, total):
        @pl.when(has_s)
        def _():
            to_north(g).wait_recv()

        @pl.when(has_n)
        def _():
            to_south(g).wait_recv()

        prow = pl.ds(pl.multiple_of(g * 8, 8), 8)
        beside = jnp.where(from_west, pack_w[prow, :], pack_e[prow, :])
        for k in range(FPG):
            f = g * FPG + k
            speed, growth, weight = wave[3 * f], wave[3 * f + 1], wave[3 * f + 2]
            base = g * GROUP_ROWS + k * ND * ROWS
            for j in range(VPF):
                at = slice(8 * j, 8 * j + 8)
                rows = pl.ds(pl.multiple_of(base + 8 * j, 8), 8)
                x = xv[rows, :] * sea_t
                halo = pltpu.roll(beside, LANES - (4 * (k * VPF + j) + 2), 1)
                w1, w2 = jnp.where(lane == LANES - 1, halo, x), jnp.where(lane >= LANES - 2, halo, x)
                e1, e2 = jnp.where(lane == 0, halo, x), jnp.where(lane < 2, halo, x)
                c = speed * cct[at, :]
                fw, fe = two_faces(
                    c + c_west, c + c_east,
                    pltpu.roll(w2, 2, 1), pltpu.roll(w1, 1, 1), x, pltpu.roll(e1, LANES - 1, 1), pltpu.roll(e2, LANES - 2, 1),
                )
                xs = south[rows, :] * sea_s
                xn = north[rows, :] * sea_n
                below = pair(pltpu.roll(xs, 7, 0), pltpu.roll(x, 1, 0))
                above = pair(pltpu.roll(x, 7, 0), pltpu.roll(xn, 1, 0))
                c = speed * trig_ref[1, at, :]
                fs, fn = two_faces(c + c_south, c + c_north, xs, below, x, above, xn)
                out = x - 0.5 * (fe - fw) - (metric_b * fn - metric_a * fs)
                pbuf[k, 8 + 8 * j : 16 + 8 * j, :] = out
                if j == 0:
                    pbuf[k, 8 + ND * ROWS : 16 + ND * ROWS, :] = out
                if j == VPF - 1:
                    pbuf[k, 0:8, :] = out
            for j in range(VPF):
                at = slice(8 * j, 8 * j + 8)
                o = 8 + 8 * j
                low2, low, mid, high = (pbuf[k, o + i : o + i + 8, :] for i in (-4, -2, 0, 2))
                d0, d1, d2 = low - low2, mid - low, high - mid
                flux = face(speed * tnt[at, :], low, mid, d1, d1 - d0, d2 - d1)
                fbuf[k, at, :] = flux
                if j == 0:
                    fbuf[k, ND * ROWS : ND * ROWS + 8, :] = flux
            square_sum = jnp.zeros((8, LANES), jnp.float32)
            for j in range(VPF):
                at = slice(8 * j, 8 * j + 8)
                rows = pl.ds(pl.multiple_of(base + 8 * j, 8), 8)
                turned = pbuf[k, 8 + 8 * j : 16 + 8 * j, :] - 0.5 * (fbuf[k, 8 * j + 2 : 8 * j + 10, :] - fbuf[k, at, :])
                square_sum = square_sum + turned * turned
                av[rows, :] = (sea_t * turned) * jnp.maximum(growth * wnd[at, :] + (1.0 - GROWTH), 1.0)
            total = total + weight * square_sum
        return total

    total = lax.fori_loop(0, GROUPS, group, jnp.zeros((8, LANES), jnp.float32))
    total = total + pltpu.roll(total, 4, 0)
    total = (total + pltpu.roll(total, 2, 0)) * (2.0 / (NF * ND))
    for f in range(NF):
        damp_ref[f] = 1.0 / (1.0 + total * ((f + 1.0) / NF))

    def finish(g, carry):
        @pl.when(has_n)
        def _():
            to_north(g).wait_send()

        @pl.when(has_s)
        def _():
            to_south(g).wait_send()

        return carry

    lax.fori_loop(0, GROUPS, finish, 0)
    for d in range(1, bands):
        msg_copy(d, b).wait_send()

    @pl.when(b == bands - 1)
    def _():
        for t in range(bands):
            edge_copy(t, True).wait_send()

    @pl.when(b == 0)
    def _():
        for t in range(bands):
            edge_copy(t, False).wait_send()

    pack_copy(True).wait_send()
    pack_copy(False).wait_send()

    @pl.when(has_n)
    def _():
        mask_copy(True).wait_send()

    @pl.when(has_s)
    def _():
        mask_copy(False).wait_send()


def damped(a_ref, damp_ref, o_hbm, ov, sem):
    for g in range(GROUPS):
        at = pl.ds(g * GROUP_ROWS, GROUP_ROWS)
        for k in range(FPG):
            factor = damp_ref[g * FPG + k]
            for j in range(VPF):
                rows = slice(g * GROUP_ROWS + 8 * (k * VPF + j), g * GROUP_ROWS + 8 * (k * VPF + j) + 8)
                ov[rows, :] = a_ref[rows, :] * factor
        pltpu.make_async_copy(ov.at[at], o_hbm.at[at], sem.at[g]).start()
    for g in range(GROUPS):
        at = pl.ds(g * GROUP_ROWS, GROUP_ROWS)
        pltpu.make_async_copy(ov.at[at], o_hbm.at[at], sem.at[g]).wait()


def per_device(bands, specs, spectra, sea_mask, wind, current):
    rows_all = ROWS_ALL
    geo, wave, trig = tables(bands)
    f32 = jnp.float32
    vmem = pl.BlockSpec(memory_space=pltpu.VMEM)
    hbm = pl.BlockSpec(memory_space=pl.ANY)
    dma = pltpu.SemaphoreType.DMA
    grown, damp = pl.pallas_call(
        functools.partial(kernel, bands, specs),
        out_shape=(
            pltpu.VMEM((rows_all, LANES), f32),
            pltpu.VMEM((NF, 8, LANES), f32),
        ),
        in_specs=[hbm] * 7,
        out_specs=(vmem, vmem),
        scratch_shapes=[
            pltpu.SMEM(geo.shape, f32),
            pltpu.SMEM(wave.shape, f32),
            pltpu.VMEM((ROWS, LANES), jnp.int32),
            pltpu.VMEM((2, LANES // bands, bands * ROWS), f32),
            pltpu.VMEM((2, LANES // bands, bands * ROWS), f32),
            pltpu.VMEM(trig.shape, f32),
            dma((6,)),
            pltpu.VMEM((rows_all, LANES), f32),
            pltpu.VMEM((rows_all, LANES), f32),
            pltpu.VMEM((rows_all, LANES), f32),
            pltpu.VMEM((ROWS, LANES), jnp.int32),
            pltpu.VMEM((ROWS, LANES), jnp.int32),
            pltpu.VMEM((LANES, LANES), f32),
            pltpu.VMEM((48, LANES), f32),
            pltpu.VMEM((bands, 1, LANES), f32),
            pltpu.VMEM((bands, 1, LANES), f32),
            pltpu.VMEM((1, LANES), f32),
            pltpu.VMEM((1, LANES), f32),
            pltpu.VMEM((GROUPS * 8, LANES), f32),
            pltpu.VMEM((GROUPS * 8, LANES), f32),
            pltpu.VMEM((GROUPS * 8, LANES), f32),
            pltpu.VMEM((ND * ROWS, LANES), f32),
            pltpu.VMEM((ND * ROWS, LANES), f32),
            pltpu.VMEM((ND * ROWS, LANES), f32),
            pltpu.VMEM((FPG, ND * ROWS + 16, LANES), f32),
            pltpu.VMEM((FPG, ND * ROWS + 8, LANES), f32),
            dma(()), dma((bands,)), dma((bands,)), dma((bands,)), dma((2,)),
            dma((2,)), dma((2,)), dma((2,)), dma((2,)),
            dma((GROUPS,)), dma((GROUPS,)), dma((GROUPS,)), dma((GROUPS,)),
        ],
        compiler_params=pltpu.CompilerParams(collective_id=0, has_side_effects=True),
        name="wave_step",
    )(
        jnp.asarray(geo), jnp.asarray(wave),
        spectra.reshape(rows_all, LANES), sea_mask,
        wind.transpose(0, 2, 1), current.transpose(0, 2, 1), jnp.asarray(trig),
    )
    out = pl.pallas_call(
        damped,
        out_shape=jax.ShapeDtypeStruct((rows_all, LANES), f32),
        in_specs=[vmem, vmem],
        out_specs=hbm,
        scratch_shapes=[pltpu.VMEM((rows_all, LANES), f32), dma((GROUPS,))],
        name="damped",
    )(*(pltpu.with_memory_space_constraint(v, pltpu.VMEM) for v in (grown, damp)))
    return out.reshape(NF * ND, ROWS, LANES)


def solution(mesh):
    placed = (
        P(None, "band", "spec"),
        P("band", "spec"),
        P(None, None, ("spec", "band")),
        P(None, None, ("spec", "band")),
    )
    return jax.shard_map(
        functools.partial(per_device, mesh.shape["band"], mesh.shape["spec"]),
        mesh=mesh, in_specs=placed, out_specs=P(None, "band", "spec"), check_vma=False,
    )
```

```python
import functools
import math

import jax
import jax.numpy as jnp
import numpy as np
from jax import lax
from jax.experimental import pallas as pl
from jax.experimental.pallas import tpu as pltpu
from jax.sharding import PartitionSpec as P

NF = 36
ND = 36

LAT_SOUTH = 30.0
LAT_NORTH = 55.0
SPEED_TOP = 0.35
FREQ_STEP = 1.1
TURNING = 1.5
GROWTH = 0.05
WIND_COUPLING = 0.04

MESH = pl.DeviceIdType.MESH
LANES = 128
ROWS = 2
VPF = ND * ROWS // 8
FPG = 3
GROUPS = NF // FPG
GROUP_ROWS = FPG * ND * ROWS
ROWS_ALL = NF * ND * ROWS
FIRST_PART = 4


def tables(bands):
    total = bands * ROWS
    rad = math.pi / 180.0

    def lat(p):
        return (LAT_SOUTH + (LAT_NORTH - LAT_SOUTH) * p / total) * rad

    geo = np.zeros((bands, 8), np.float64)
    for b in range(bands):
        y = b * ROWS
        c0, c1 = math.cos(lat(y + 0.5)), math.cos(lat(y + 1.5))
        fs, fm, fn = math.cos(lat(y)), math.cos(lat(y + 1)), math.cos(lat(y + 2))
        geo[b] = [
            1.0 / c0, 1.0 / c1,
            0.5 * fs / c0, 0.5 * fm / c1,
            0.5 * fm / c0, 0.5 * fn / c1,
            math.tan(lat(y + 0.5)), math.tan(lat(y + 1.5)),
        ]
    f = np.arange(NF)
    speed = SPEED_TOP * FREQ_STEP ** (-f)
    wave = np.stack([speed, GROWTH * WIND_COUPLING * FREQ_STEP**f, (f + 1.0) / NF], 1)
    theta = 2.0 * math.pi * np.arange(ND) / ND
    cos, sin = np.cos(theta), np.sin(theta)
    turn = -TURNING * 0.5 * (np.roll(cos, 1) + cos)

    def spread(v):
        return np.broadcast_to(np.repeat(v, ROWS)[:, None], (ND * ROWS, LANES))

    trig = np.stack([spread(cos), spread(sin), spread(turn)]).astype(np.float32)
    return geo.astype(np.float32).reshape(-1), wave.astype(np.float32).reshape(-1), trig


def face(c, low, high, step, bend_low, bend_high):
    bend = jnp.where(c >= 0.0, bend_low, bend_high)
    return c * (((low + high) - c * step) + (c * c * (1.0 / 3.0) - 1.0 / 3.0) * bend)


def two_faces(c_low, c_high, low2, low, mid, high, high2):
    d0, d1, d2, d3 = low - low2, mid - low, high - mid, high2 - high
    k0, k1, k2 = d1 - d0, d2 - d1, d3 - d2
    return face(c_low, low, mid, d1, k0, k1), face(c_high, mid, high, d2, k1, k2)


def kernel(
    bands, specs,
    geo_hbm, wave_hbm, x_hbm, mask_hbm, wind_hbm, cur_hbm, trig_hbm,
    av, damp_ref,
    geo, wave, mask_ref, wind_ref, cur_ref, trig_ref, small_sem,
    xv, south, north, mask_s, mask_n, square, strip, out_raw, out_msg, in_msg, edge_in,
    pack, pack_w, pack_e, cct, tnt, wnd, pbuf, fbuf,
    x_sem, msg_send, msg_recv, edge_sem, tokens, late, pack_send, pack_recv, mask_send, mask_recv,
    n_send, s_send, n_recv, s_recv,
):
    b = lax.axis_index("band")
    s = lax.axis_index("spec")
    west, east = lax.rem(s + specs - 1, specs), lax.rem(s + 1, specs)
    has_n, has_s = b < bands - 1, b > 0
    up_band, down_band = jnp.minimum(b + 1, bands - 1), jnp.maximum(b - 1, 0)
    cols = LANES // bands

    barrier = pltpu.get_barrier_semaphore()
    first_col, last_col = s == 0, s == specs - 1
    pl.semaphore_signal(barrier, inc=1, device_id=(b, west), device_id_type=MESH)

    @pl.when(jnp.logical_not(last_col))
    def _():
        pl.semaphore_signal(barrier, inc=1, device_id=(b, east), device_id_type=MESH)

    def say(sem, target):
        pl.semaphore_signal(sem, inc=1, device_id=(target, s), device_id_type=MESH)

    partners = [b + bit - 2 * bit * lax.rem(b // bit, 2) for bit in (1, 2, 4, 8)]
    for target in partners:
        say(barrier, target)

    odd = lax.rem(b, 2) == 1

    @pl.when(odd & has_n)
    def _():
        say(barrier, up_band)

    @pl.when(jnp.logical_not(odd) & has_s)
    def _():
        say(barrier, down_band)

    small = [
        pltpu.make_async_copy(a, v, small_sem.at[i])
        for i, (a, v) in enumerate((
            (wind_hbm, wind_ref), (cur_hbm, cur_ref), (mask_hbm, mask_ref),
            (geo_hbm, geo), (wave_hbm, wave), (trig_hbm, trig_ref),
        ))
    ]
    for copy in small[:3]:
        copy.start()
    load = pltpu.make_async_copy(x_hbm, xv, x_sem)
    load.start()
    for copy in small[3:]:
        copy.start()

    sub = lax.broadcasted_iota(jnp.int32, (8, LANES), 0)
    lane = lax.broadcasted_iota(jnp.int32, (8, LANES), 1)
    even = lax.rem(sub, 2) == 0

    def pair(a, c):
        return jnp.where(even, a, c)

    square[...] = jnp.zeros_like(square)
    for copy in small[:3]:
        copy.wait()
    for i in range(2):
        square[i * 8 : i * 8 + cols, 0 : bands * ROWS] = wind_ref[i]
        square[16 + i * 8 : 16 + i * 8 + cols, 0 : bands * ROWS] = cur_ref[i]
    strip[...] = jnp.zeros_like(strip)
    strip[8 : 8 + bands * ROWS, :] = square[...].T[0 : bands * ROWS, :]
    message = strip[pl.ds(8, bands, stride=2), :]
    for q, first in ((1, 9), (2, 7), (3, 10)):
        message = message + pltpu.roll(strip[pl.ds(first, bands, stride=2), :], 32 * q, 1)
    for d in range(bands):
        out_raw[d] = message[d : d + 1]
        out_msg[d] = message[d : d + 1]

    sea = mask_ref[...].astype(jnp.float32)
    sea_t = pair(sea[0:1], sea[1:2])

    load.wait()

    def pack_group(g, carry):
        acc = jnp.zeros((8, LANES), jnp.float32)
        for i in range(FPG * VPF):
            v = xv[pl.ds(pl.multiple_of(g * GROUP_ROWS + 8 * i, 8), 8), :] * sea_t
            acc = jnp.where((lane >= 4 * i) & (lane < 4 * i + 4), pltpu.roll(v, 4 * i + 2, 1), acc)
        pack[pl.ds(pl.multiple_of(g * 8, 8), 8), :] = acc
        return carry

    lax.fori_loop(0, GROUPS, pack_group, 0)

    at_end = (b == 0) | (b == bands - 1)

    greeted = 7 - jnp.where(at_end, 1, 0) - jnp.where(first_col, 1, 0)
    pl.semaphore_wait(barrier, greeted)

    @pl.when(last_col)
    def _():
        pl.semaphore_signal(late.at[0], inc=1, device_id=(b, 0), device_id_type=MESH)

    edge_to_east = pltpu.make_async_remote_copy(
        src_ref=out_raw, dst_ref=edge_in, send_sem=edge_sem.at[0], recv_sem=edge_sem.at[1],
        device_id=(b, east), device_id_type=MESH,
    )
    edge_to_west = pltpu.make_async_remote_copy(
        src_ref=out_raw, dst_ref=edge_in, send_sem=edge_sem.at[0], recv_sem=edge_sem.at[1],
        device_id=(b, west), device_id_type=MESH,
    )

    @pl.when(b == bands - 1)
    def _():
        edge_to_east.start()

    @pl.when((b == 0) & jnp.logical_not(first_col))
    def _():
        edge_to_west.start()

    def chunk(g):
        return pl.ds(pl.multiple_of(g * GROUP_ROWS, GROUP_ROWS), GROUP_ROWS)

    def to_north(g):
        return pltpu.make_async_remote_copy(
            src_ref=x_hbm.at[chunk(g)], dst_ref=south.at[chunk(g)], send_sem=n_send.at[g], recv_sem=s_recv.at[g],
            device_id=(up_band, s), device_id_type=MESH,
        )

    def to_south(g):
        return pltpu.make_async_remote_copy(
            src_ref=x_hbm.at[chunk(g)], dst_ref=north.at[chunk(g)], send_sem=s_send.at[g], recv_sem=n_recv.at[g],
            device_id=(down_band, s), device_id_type=MESH,
        )

    def mask_copy(northward):
        return pltpu.make_async_remote_copy(
            src_ref=mask_ref, dst_ref=mask_s if northward else mask_n,
            send_sem=mask_send.at[0 if northward else 1], recv_sem=mask_recv.at[0 if northward else 1],
            device_id=(up_band if northward else down_band, s), device_id_type=MESH,
        )

    def pack_copy(to_east):
        return pltpu.make_async_remote_copy(
            src_ref=pack, dst_ref=pack_w if to_east else pack_e,
            send_sem=pack_send.at[0 if to_east else 1], recv_sem=pack_recv.at[0 if to_east else 1],
            device_id=(b, east if to_east else west), device_id_type=MESH,
        )

    @pl.when(has_n)
    def _():
        mask_copy(True).start()

    @pl.when(has_s)
    def _():
        mask_copy(False).start()

    pack_copy(True).start()

    @pl.when(jnp.logical_not(first_col))
    def _():
        pack_copy(False).start()

    def send_chunk(g, carry):
        @pl.when(has_n)
        def _():
            to_north(g).start()

        @pl.when(has_s)
        def _():
            to_south(g).start()

        return carry

    lax.fori_loop(0, FIRST_PART, send_chunk, 0)

    for i in range(3):
        say(tokens.at[i], partners[i])
        pl.semaphore_wait(tokens.at[i], 1)

    def msg_copy(target, source):
        return pltpu.make_async_remote_copy(
            src_ref=out_msg.at[target], dst_ref=in_msg.at[source],
            send_sem=msg_send.at[target], recv_sem=msg_recv.at[source],
            device_id=(target, s), device_id_type=MESH,
        )

    @pl.when(at_end)
    def _():
        edge_to_east.wait_recv()
        edge = jnp.concatenate([edge_in[d] for d in range(bands)], axis=0)
        wide = lax.broadcasted_iota(jnp.int32, (bands, LANES), 1)
        last = (lax.broadcasted_iota(jnp.int32, (bands, LANES), 0) * 0 + b) > 0
        first_row = jnp.where(last, pltpu.roll(edge, 64 - (16 + cols - 1), 1), pltpu.roll(edge, 64 - 16, 1))
        second_row = jnp.where(last, pltpu.roll(edge, 65 - (48 + cols - 1), 1), pltpu.roll(edge, 65 - 48, 1))
        plain = jnp.concatenate([out_raw[d] for d in range(bands)], axis=0)
        merged = jnp.where(wide == 64, first_row, jnp.where(wide == 65, second_row, plain))
        for d in range(bands):
            out_msg[d] = merged[d : d + 1]

    for d in range(1, bands):
        msg_copy(lax.rem(b + d, bands), b).start()

    @pl.when(first_col)
    def _():
        pl.semaphore_wait(late.at[0], 1)

        @pl.when(b == 0)
        def _():
            edge_to_west.start()

        pack_copy(False).start()

    lax.fori_loop(FIRST_PART, GROUPS, send_chunk, 0)

    @pl.when(b == 0)
    def _():
        mask_s[...] = jnp.zeros_like(mask_s)

        def clear(i, carry):
            south[pl.ds(pl.multiple_of(i * GROUP_ROWS, 8), GROUP_ROWS), :] = jnp.zeros((GROUP_ROWS, LANES), jnp.float32)
            return carry

        lax.fori_loop(0, GROUPS, clear, 0)

    @pl.when(b == bands - 1)
    def _():
        mask_n[...] = jnp.zeros_like(mask_n)

        def clear(i, carry):
            north[pl.ds(pl.multiple_of(i * GROUP_ROWS, 8), GROUP_ROWS), :] = jnp.zeros((GROUP_ROWS, LANES), jnp.float32)
            return carry

        lax.fori_loop(0, GROUPS, clear, 0)

    for copy in small[3:]:
        copy.wait()
    g0 = b * 8
    inv_cos = pair(geo[g0], geo[g0 + 1])
    metric_a = pair(geo[g0 + 2], geo[g0 + 3])
    metric_b = pair(geo[g0 + 4], geo[g0 + 5])
    tangent = pair(geo[g0 + 6], geo[g0 + 7])
    for j in range(VPF):
        at = slice(8 * j, 8 * j + 8)
        cct[at, :] = trig_ref[0, at, :] * inv_cos
        tnt[at, :] = trig_ref[2, at, :] * tangent

    in_msg[b] = out_msg[b]
    for d in range(1, bands):
        msg_copy(b, lax.rem(b + d, bands)).wait_recv()

    got = jnp.concatenate(
        [
            pltpu.roll(jnp.concatenate([in_msg[h + d] for d in range(8)], axis=0), h * cols, 1, stride=cols, stride_axis=0)
            for h in range(0, bands, 8)
        ],
        axis=0,
    )
    own = lax.broadcasted_iota(jnp.int32, (bands, LANES), 1) // cols == lax.broadcasted_iota(jnp.int32, (bands, LANES), 0)

    def field(q, f):
        moved = pltpu.roll(got, (LANES - 32 * q - 8 * f) % LANES, 1)
        return jnp.sum(jnp.where(own, moved, 0.0), axis=0, keepdims=True)

    w0 = pair(field(0, 0), field(1, 0))
    w1 = pair(field(0, 1), field(1, 1))
    u = pair(field(0, 2), field(1, 2))
    v0, v1, vs, vn = field(0, 3), field(1, 3), field(2, 3), field(3, 3)
    wm = jnp.broadcast_to(in_msg[bands - 1], (8, LANES))
    em = jnp.broadcast_to(in_msg[0], (8, LANES))
    u_w = pair(pltpu.roll(wm, LANES - 1 - 64, 1), pltpu.roll(wm, LANES - 1 - 65, 1))
    u_e = pair(pltpu.roll(em, LANES - 64, 1), pltpu.roll(em, LANES - 65, 1))
    c_west = 0.5 * (u + pltpu.roll(jnp.where(lane == LANES - 1, u_w, u), 1, 1))
    c_east = 0.5 * (u + pltpu.roll(jnp.where(lane == 0, u_e, u), LANES - 1, 1))
    c_south = 0.5 * pair(vs + v0, v0 + v1)
    c_north = 0.5 * pair(v0 + v1, v1 + vn)
    for j in range(VPF):
        at = slice(8 * j, 8 * j + 8)
        wnd[at, :] = w0 * trig_ref[0, at, :] + w1 * trig_ref[1, at, :]

    pack_copy(True).wait_recv()
    pack_copy(False).wait_recv()

    @pl.when(has_s)
    def _():
        mask_copy(True).wait_recv()

    @pl.when(has_n)
    def _():
        mask_copy(False).wait_recv()

    ms, mn = mask_s[...].astype(jnp.float32), mask_n[...].astype(jnp.float32)
    sea_s = pair(ms[0:1], ms[1:2])
    sea_n = pair(mn[0:1], mn[1:2])
    from_west = lax.rem(lane, 4) < 2

    def group(g, total):
        @pl.when(has_s)
        def _():
            to_north(g).wait_recv()

        @pl.when(has_n)
        def _():
            to_south(g).wait_recv()

        prow = pl.ds(pl.multiple_of(g * 8, 8), 8)
        beside = jnp.where(from_west, pack_w[prow, :], pack_e[prow, :])
        for k in range(FPG):
            f = g * FPG + k
            speed, growth, weight = wave[3 * f], wave[3 * f + 1], wave[3 * f + 2]
            base = g * GROUP_ROWS + k * ND * ROWS
            for j in range(VPF):
                at = slice(8 * j, 8 * j + 8)
                rows = pl.ds(pl.multiple_of(base + 8 * j, 8), 8)
                x = xv[rows, :] * sea_t
                halo = pltpu.roll(beside, LANES - (4 * (k * VPF + j) + 2), 1)
                w1, w2 = jnp.where(lane == LANES - 1, halo, x), jnp.where(lane >= LANES - 2, halo, x)
                e1, e2 = jnp.where(lane == 0, halo, x), jnp.where(lane < 2, halo, x)
                c = speed * cct[at, :]
                fw, fe = two_faces(
                    c + c_west, c + c_east,
                    pltpu.roll(w2, 2, 1), pltpu.roll(w1, 1, 1), x, pltpu.roll(e1, LANES - 1, 1), pltpu.roll(e2, LANES - 2, 1),
                )
                xs = south[rows, :] * sea_s
                xn = north[rows, :] * sea_n
                below = pair(pltpu.roll(xs, 7, 0), pltpu.roll(x, 1, 0))
                above = pair(pltpu.roll(x, 7, 0), pltpu.roll(xn, 1, 0))
                c = speed * trig_ref[1, at, :]
                fs, fn = two_faces(c + c_south, c + c_north, xs, below, x, above, xn)
                out = x - 0.5 * (fe - fw) - (metric_b * fn - metric_a * fs)
                pbuf[k, 8 + 8 * j : 16 + 8 * j, :] = out
                if j == 0:
                    pbuf[k, 8 + ND * ROWS : 16 + ND * ROWS, :] = out
                if j == VPF - 1:
                    pbuf[k, 0:8, :] = out
            for j in range(VPF):
                at = slice(8 * j, 8 * j + 8)
                o = 8 + 8 * j
                low2, low, mid, high = (pbuf[k, o + i : o + i + 8, :] for i in (-4, -2, 0, 2))
                d0, d1, d2 = low - low2, mid - low, high - mid
                flux = face(speed * tnt[at, :], low, mid, d1, d1 - d0, d2 - d1)
                fbuf[k, at, :] = flux
                if j == 0:
                    fbuf[k, ND * ROWS : ND * ROWS + 8, :] = flux
            square_sum = jnp.zeros((8, LANES), jnp.float32)
            for j in range(VPF):
                at = slice(8 * j, 8 * j + 8)
                rows = pl.ds(pl.multiple_of(base + 8 * j, 8), 8)
                turned = pbuf[k, 8 + 8 * j : 16 + 8 * j, :] - 0.5 * (fbuf[k, 8 * j + 2 : 8 * j + 10, :] - fbuf[k, at, :])
                square_sum = square_sum + turned * turned
                av[rows, :] = (sea_t * turned) * jnp.maximum(growth * wnd[at, :] + (1.0 - GROWTH), 1.0)
            total = total + weight * square_sum
        return total

    total = lax.fori_loop(0, GROUPS, group, jnp.zeros((8, LANES), jnp.float32))
    total = total + pltpu.roll(total, 4, 0)
    total = (total + pltpu.roll(total, 2, 0)) * (2.0 / (NF * ND))
    for f in range(NF):
        damp_ref[f] = 1.0 / (1.0 + total * ((f + 1.0) / NF))

    def finish(g, carry):
        @pl.when(has_n)
        def _():
            to_north(g).wait_send()

        @pl.when(has_s)
        def _():
            to_south(g).wait_send()

        return carry

    lax.fori_loop(0, GROUPS, finish, 0)
    for d in range(1, bands):
        msg_copy(lax.rem(b + d, bands), b).wait_send()

    @pl.when(at_end)
    def _():
        edge_to_east.wait_send()

    pack_copy(True).wait_send()
    pack_copy(False).wait_send()

    @pl.when(has_n)
    def _():
        mask_copy(True).wait_send()

    @pl.when(has_s)
    def _():
        mask_copy(False).wait_send()


def damped(a_ref, damp_ref, o_hbm, ov, sem):
    for g in range(GROUPS):
        at = pl.ds(g * GROUP_ROWS, GROUP_ROWS)
        for k in range(FPG):
            factor = damp_ref[g * FPG + k]
            for j in range(VPF):
                rows = slice(g * GROUP_ROWS + 8 * (k * VPF + j), g * GROUP_ROWS + 8 * (k * VPF + j) + 8)
                ov[rows, :] = a_ref[rows, :] * factor
        pltpu.make_async_copy(ov.at[at], o_hbm.at[at], sem.at[g]).start()
    for g in range(GROUPS):
        at = pl.ds(g * GROUP_ROWS, GROUP_ROWS)
        pltpu.make_async_copy(ov.at[at], o_hbm.at[at], sem.at[g]).wait()


def per_device(bands, specs, spectra, sea_mask, wind, current):
    rows_all = ROWS_ALL
    geo, wave, trig = tables(bands)
    f32 = jnp.float32
    vmem = pl.BlockSpec(memory_space=pltpu.VMEM)
    hbm = pl.BlockSpec(memory_space=pl.ANY)
    dma = pltpu.SemaphoreType.DMA
    token = pltpu.SemaphoreType.REGULAR
    grown, damp = pl.pallas_call(
        functools.partial(kernel, bands, specs),
        out_shape=(
            pltpu.VMEM((rows_all, LANES), f32),
            pltpu.VMEM((NF, 8, LANES), f32),
        ),
        in_specs=[hbm] * 7,
        out_specs=(vmem, vmem),
        scratch_shapes=[
            pltpu.SMEM(geo.shape, f32),
            pltpu.SMEM(wave.shape, f32),
            pltpu.VMEM((ROWS, LANES), jnp.int32),
            pltpu.VMEM((2, LANES // bands, bands * ROWS), f32),
            pltpu.VMEM((2, LANES // bands, bands * ROWS), f32),
            pltpu.VMEM(trig.shape, f32),
            dma((6,)),
            pltpu.VMEM((rows_all, LANES), f32),
            pltpu.VMEM((rows_all, LANES), f32),
            pltpu.VMEM((rows_all, LANES), f32),
            pltpu.VMEM((ROWS, LANES), jnp.int32),
            pltpu.VMEM((ROWS, LANES), jnp.int32),
            pltpu.VMEM((LANES, LANES), f32),
            pltpu.VMEM((48, LANES), f32),
            pltpu.VMEM((bands, 1, LANES), f32),
            pltpu.VMEM((bands, 1, LANES), f32),
            pltpu.VMEM((bands, 1, LANES), f32),
            pltpu.VMEM((bands, 1, LANES), f32),
            pltpu.VMEM((GROUPS * 8, LANES), f32),
            pltpu.VMEM((GROUPS * 8, LANES), f32),
            pltpu.VMEM((GROUPS * 8, LANES), f32),
            pltpu.VMEM((ND * ROWS, LANES), f32),
            pltpu.VMEM((ND * ROWS, LANES), f32),
            pltpu.VMEM((ND * ROWS, LANES), f32),
            pltpu.VMEM((FPG, ND * ROWS + 16, LANES), f32),
            pltpu.VMEM((FPG, ND * ROWS + 8, LANES), f32),
            dma(()), dma((bands,)), dma((bands,)), dma((2,)), token((3,)), token((1,)),
            dma((2,)), dma((2,)), dma((2,)), dma((2,)),
            dma((GROUPS,)), dma((GROUPS,)), dma((GROUPS,)), dma((GROUPS,)),
        ],
        compiler_params=pltpu.CompilerParams(collective_id=0, has_side_effects=True),
        name="wave_step",
    )(
        jnp.asarray(geo), jnp.asarray(wave),
        spectra.reshape(rows_all, LANES), sea_mask,
        wind.transpose(0, 2, 1), current.transpose(0, 2, 1), jnp.asarray(trig),
    )
    out = pl.pallas_call(
        damped,
        out_shape=jax.ShapeDtypeStruct((rows_all, LANES), f32),
        in_specs=[vmem, vmem],
        out_specs=hbm,
        scratch_shapes=[pltpu.VMEM((rows_all, LANES), f32), dma((GROUPS,))],
        name="damped",
    )(*(pltpu.with_memory_space_constraint(v, pltpu.VMEM) for v in (grown, damp)))
    return out.reshape(NF * ND, ROWS, LANES)


def solution(mesh):
    placed = (
        P(None, "band", "spec"),
        P("band", "spec"),
        P(None, None, ("spec", "band")),
        P(None, None, ("spec", "band")),
    )
    return jax.shard_map(
        functools.partial(per_device, mesh.shape["band"], mesh.shape["spec"]),
        mesh=mesh, in_specs=placed, out_specs=P(None, "band", "spec"), check_vma=False,
    )
```

```python
import functools
import math

import jax
import jax.numpy as jnp
import numpy as np
from jax import lax
from jax.experimental import pallas as pl
from jax.experimental.pallas import tpu as pltpu
from jax.sharding import PartitionSpec as P

NF = 36
ND = 36

LAT_SOUTH = 30.0
LAT_NORTH = 55.0
SPEED_TOP = 0.35
FREQ_STEP = 1.1
TURNING = 1.5
GROWTH = 0.05
WIND_COUPLING = 0.04

MESH = pl.DeviceIdType.MESH
LANES = 128
ROWS = 2
VPF = ND * ROWS // 8
FPG = 3
GROUPS = NF // FPG
GROUP_ROWS = FPG * ND * ROWS
ROWS_ALL = NF * ND * ROWS
PARTS = (5, 3, 2, 1, 1)
FIRST_PART = 1


def tables(bands):
    total = bands * ROWS
    rad = math.pi / 180.0

    def lat(p):
        return (LAT_SOUTH + (LAT_NORTH - LAT_SOUTH) * p / total) * rad

    geo = np.zeros((bands, 8), np.float64)
    for b in range(bands):
        y = b * ROWS
        c0, c1 = math.cos(lat(y + 0.5)), math.cos(lat(y + 1.5))
        fs, fm, fn = math.cos(lat(y)), math.cos(lat(y + 1)), math.cos(lat(y + 2))
        geo[b] = [
            1.0 / c0, 1.0 / c1,
            0.5 * fs / c0, 0.5 * fm / c1,
            0.5 * fm / c0, 0.5 * fn / c1,
            math.tan(lat(y + 0.5)), math.tan(lat(y + 1.5)),
        ]
    f = np.arange(NF)
    speed = SPEED_TOP * FREQ_STEP ** (-f)
    wave = np.stack([speed, GROWTH * WIND_COUPLING * FREQ_STEP**f, (f + 1.0) / NF], 1)
    theta = 2.0 * math.pi * np.arange(ND) / ND
    cos, sin = np.cos(theta), np.sin(theta)
    turn = -TURNING * 0.5 * (np.roll(cos, 1) + cos)

    def spread(v):
        return np.broadcast_to(np.repeat(v, ROWS)[:, None], (ND * ROWS, LANES))

    trig = np.stack([spread(cos), spread(sin), spread(turn)]).astype(np.float32)
    return geo.astype(np.float32).reshape(-1), wave.astype(np.float32).reshape(-1), trig


def face(c, low, high, step, bend_low, bend_high):
    bend = jnp.where(c >= 0.0, bend_low, bend_high)
    return c * (((low + high) - c * step) + (c * c * (1.0 / 3.0) - 1.0 / 3.0) * bend)


def two_faces(c_low, c_high, low2, low, mid, high, high2):
    d0, d1, d2, d3 = low - low2, mid - low, high - mid, high2 - high
    k0, k1, k2 = d1 - d0, d2 - d1, d3 - d2
    return face(c_low, low, mid, d1, k0, k1), face(c_high, mid, high, d2, k1, k2)


def kernel(
    bands, specs,
    geo_hbm, wave_hbm, x_hbm, mask_hbm, wind_hbm, cur_hbm, trig_hbm,
    av, damp_ref,
    geo, wave, mask_ref, wind_ref, cur_ref, trig_ref, small_sem,
    xv, south, north, mask_s, mask_n, square, strip, out_raw, out_msg, in_msg, edge_in, far_edge,
    pack, go_east, go_west, pack_w, pack_e, cct, tnt, wnd, pbuf, fbuf,
    x_sem, msg_send, msg_recv, edge_sem, far_send, tokens, late, pack_send, pack_recv, mask_send, mask_recv,
    n_send, s_send, n_recv, s_recv,
):
    b = lax.axis_index("band")
    s = lax.axis_index("spec")
    west, east = lax.rem(s + specs - 1, specs), lax.rem(s + 1, specs)
    has_n, has_s = b < bands - 1, b > 0
    up_band, down_band = jnp.minimum(b + 1, bands - 1), jnp.maximum(b - 1, 0)
    cols = LANES // bands

    barrier = pltpu.get_barrier_semaphore()
    first_col, last_col = s == 0, s == specs - 1
    pl.semaphore_signal(barrier, inc=1, device_id=(b, west), device_id_type=MESH)

    @pl.when(jnp.logical_not(last_col))
    def _():
        pl.semaphore_signal(barrier, inc=1, device_id=(b, east), device_id_type=MESH)

    def say(sem, target):
        pl.semaphore_signal(sem, inc=1, device_id=(target, s), device_id_type=MESH)

    partners = [b + bit - 2 * bit * lax.rem(b // bit, 2) for bit in (1, 2, 4, 8)]
    has_bit = [lax.rem(b // bit, 2) == 1 for bit in (1, 2, 4, 8)]
    say(barrier, partners[0])
    for i in range(1, 4):

        @pl.when(jnp.logical_not(has_bit[i]))
        def _(i=i):
            say(barrier, partners[i])

    odd = lax.rem(b, 2) == 1

    @pl.when(odd & has_n)
    def _():
        say(barrier, up_band)

    @pl.when(jnp.logical_not(odd) & has_s)
    def _():
        say(barrier, down_band)

    @pl.when(first_col & (b < bands - 1))
    def _():
        pl.semaphore_signal(barrier, inc=1, device_id=(bands - 1, west), device_id_type=MESH)

    small = [
        pltpu.make_async_copy(a, v, small_sem.at[i])
        for i, (a, v) in enumerate((
            (wind_hbm, wind_ref), (cur_hbm, cur_ref), (mask_hbm, mask_ref),
            (geo_hbm, geo), (wave_hbm, wave), (trig_hbm, trig_ref),
        ))
    ]
    for copy in small[:3]:
        copy.start()
    load = pltpu.make_async_copy(x_hbm, xv, x_sem)
    load.start()
    for copy in small[3:]:
        copy.start()

    sub = lax.broadcasted_iota(jnp.int32, (8, LANES), 0)
    lane = lax.broadcasted_iota(jnp.int32, (8, LANES), 1)
    even = lax.rem(sub, 2) == 0

    def pair(a, c):
        return jnp.where(even, a, c)

    square[...] = jnp.zeros_like(square)
    for copy in small[:3]:
        copy.wait()
    for i in range(2):
        square[i * 8 : i * 8 + cols, 0 : bands * ROWS] = wind_ref[i]
        square[16 + i * 8 : 16 + i * 8 + cols, 0 : bands * ROWS] = cur_ref[i]
    strip[...] = jnp.zeros_like(strip)
    strip[8 : 8 + bands * ROWS, :] = square[...].T[0 : bands * ROWS, :]
    message = strip[pl.ds(8, bands, stride=2), :]
    for q, first in ((1, 9), (2, 7), (3, 10)):
        message = message + pltpu.roll(strip[pl.ds(first, bands, stride=2), :], 32 * q, 1)
    for d in range(bands):
        out_raw[d] = message[d : d + 1]
        out_msg[d] = message[d : d + 1]

    sea = mask_ref[...].astype(jnp.float32)
    sea_t = pair(sea[0:1], sea[1:2])

    load.wait()

    def pack_group(g, carry):
        acc = jnp.zeros((8, LANES), jnp.float32)
        for i in range(FPG * VPF):
            v = xv[pl.ds(pl.multiple_of(g * GROUP_ROWS + 8 * i, 8), 8), :] * sea_t
            acc = jnp.where((lane >= 4 * i) & (lane < 4 * i + 4), pltpu.roll(v, 4 * i + 2, 1), acc)
        pack[pl.ds(pl.multiple_of(g * 8, 8), 8), :] = acc
        return carry

    lax.fori_loop(0, GROUPS, pack_group, 0)

    low_half = lax.rem(lane, 4) < 2
    for i in range(GROUPS // 2):
        two = [pack[16 * i + 8 * r : 16 * i + 8 * r + 8, :] for r in range(2)]
        at = slice(8 * i, 8 * i + 8)
        go_east[at, :] = jnp.where(low_half, two[0], pltpu.roll(two[1], 2, 1))
        go_west[at, :] = jnp.where(low_half, pltpu.roll(two[0], LANES - 2, 1), two[1])

    at_end = (b == 0) | (b == bands - 1)

    far_corner = last_col & (b == bands - 1)
    greeted = 4 - jnp.where(at_end, 1, 0) - jnp.where(first_col, 1, 0) + jnp.where(far_corner, bands - 1, 0)
    for i in range(1, 4):
        greeted = greeted + jnp.where(has_bit[i], 1, 0)
    pl.semaphore_wait(barrier, greeted)
    for i in range(1, 4):

        @pl.when(has_bit[i])
        def _(i=i):
            say(late.at[i], partners[i])

    @pl.when(last_col)
    def _():
        pl.semaphore_signal(late.at[0], inc=1, device_id=(b, 0), device_id_type=MESH)

    edge_to_east = pltpu.make_async_remote_copy(
        src_ref=out_raw, dst_ref=edge_in, send_sem=edge_sem.at[0], recv_sem=edge_sem.at[1],
        device_id=(b, east), device_id_type=MESH,
    )
    edge_to_west = pltpu.make_async_remote_copy(
        src_ref=out_raw, dst_ref=edge_in, send_sem=edge_sem.at[0], recv_sem=edge_sem.at[1],
        device_id=(b, west), device_id_type=MESH,
    )

    def far_copy(t):
        return pltpu.make_async_remote_copy(
            src_ref=out_raw.at[t], dst_ref=far_edge, send_sem=far_send.at[t], recv_sem=edge_sem.at[2],
            device_id=(t, 0), device_id_type=MESH,
        )

    @pl.when(far_corner)
    def _():
        for t in range(bands):
            far_copy(t).start()

    passes_east = (b == bands - 1) & jnp.logical_not(last_col)

    @pl.when(passes_east)
    def _():
        edge_to_east.start()

    @pl.when(jnp.logical_not(first_col))
    def _():
        far_edge[...] = jnp.zeros_like(far_edge)

    @pl.when((b == 0) & jnp.logical_not(first_col))
    def _():
        edge_to_west.start()

    firsts = [sum(PARTS[:i]) for i in range(len(PARTS))]

    def part(i):
        return pl.ds(firsts[i] * GROUP_ROWS, PARTS[i] * GROUP_ROWS)

    def to_north(i):
        return pltpu.make_async_remote_copy(
            src_ref=x_hbm.at[part(i)], dst_ref=south.at[part(i)], send_sem=n_send.at[i], recv_sem=s_recv.at[i],
            device_id=(up_band, s), device_id_type=MESH,
        )

    def to_south(i):
        return pltpu.make_async_remote_copy(
            src_ref=x_hbm.at[part(i)], dst_ref=north.at[part(i)], send_sem=s_send.at[i], recv_sem=n_recv.at[i],
            device_id=(down_band, s), device_id_type=MESH,
        )

    def mask_copy(northward):
        return pltpu.make_async_remote_copy(
            src_ref=mask_ref, dst_ref=mask_s if northward else mask_n,
            send_sem=mask_send.at[0 if northward else 1], recv_sem=mask_recv.at[0 if northward else 1],
            device_id=(up_band if northward else down_band, s), device_id_type=MESH,
        )

    def pack_copy(to_east):
        return pltpu.make_async_remote_copy(
            src_ref=go_east if to_east else go_west, dst_ref=pack_w if to_east else pack_e,
            send_sem=pack_send.at[0 if to_east else 1], recv_sem=pack_recv.at[0 if to_east else 1],
            device_id=(b, east if to_east else west), device_id_type=MESH,
        )

    @pl.when(has_n)
    def _():
        mask_copy(True).start()

    @pl.when(has_s)
    def _():
        mask_copy(False).start()

    pack_copy(True).start()

    @pl.when(jnp.logical_not(first_col))
    def _():
        pack_copy(False).start()

    def send_parts(some):
        for i in some:

            @pl.when(has_n)
            def _(i=i):
                to_north(i).start()

            @pl.when(has_s)
            def _(i=i):
                to_south(i).start()

    send_parts(range(FIRST_PART))

    for i in range(1, 4):

        @pl.when(jnp.logical_not(has_bit[i]))
        def _(i=i):
            pl.semaphore_wait(late.at[i], 1)

    for i in range(3):
        say(tokens.at[i], partners[i])
        pl.semaphore_wait(tokens.at[i], 1)

    def msg_copy(target, source):
        return pltpu.make_async_remote_copy(
            src_ref=out_msg.at[target], dst_ref=in_msg.at[source],
            send_sem=msg_send.at[target], recv_sem=msg_recv.at[source],
            device_id=(target, s), device_id_type=MESH,
        )

    @pl.when((b == 0) | ((b == bands - 1) & jnp.logical_not(first_col)))
    def _():
        edge_to_east.wait_recv()
        edge = jnp.concatenate([edge_in[d] for d in range(bands)], axis=0)
        wide = lax.broadcasted_iota(jnp.int32, (bands, LANES), 1)
        last = (lax.broadcasted_iota(jnp.int32, (bands, LANES), 0) * 0 + b) > 0
        first_row = jnp.where(last, pltpu.roll(edge, 64 - (16 + cols - 1), 1), pltpu.roll(edge, 64 - 16, 1))
        second_row = jnp.where(last, pltpu.roll(edge, 65 - (48 + cols - 1), 1), pltpu.roll(edge, 65 - 48, 1))
        plain = jnp.concatenate([out_raw[d] for d in range(bands)], axis=0)
        merged = jnp.where(wide == 64, first_row, jnp.where(wide == 65, second_row, plain))
        for d in range(bands):
            out_msg[d] = merged[d : d + 1]

    for d in range(1, bands):
        msg_copy(lax.rem(b + d, bands), b).start()

    @pl.when(first_col)
    def _():
        pl.semaphore_wait(late.at[0], 1)

        @pl.when(b == 0)
        def _():
            edge_to_west.start()

        pack_copy(False).start()

    send_parts(range(FIRST_PART, len(PARTS)))

    @pl.when(b == 0)
    def _():
        mask_s[...] = jnp.zeros_like(mask_s)

        def clear(i, carry):
            south[pl.ds(pl.multiple_of(i * GROUP_ROWS, 8), GROUP_ROWS), :] = jnp.zeros((GROUP_ROWS, LANES), jnp.float32)
            return carry

        lax.fori_loop(0, GROUPS, clear, 0)

    @pl.when(b == bands - 1)
    def _():
        mask_n[...] = jnp.zeros_like(mask_n)

        def clear(i, carry):
            north[pl.ds(pl.multiple_of(i * GROUP_ROWS, 8), GROUP_ROWS), :] = jnp.zeros((GROUP_ROWS, LANES), jnp.float32)
            return carry

        lax.fori_loop(0, GROUPS, clear, 0)

    for copy in small[3:]:
        copy.wait()
    g0 = b * 8
    inv_cos = pair(geo[g0], geo[g0 + 1])
    metric_a = pair(geo[g0 + 2], geo[g0 + 3])
    metric_b = pair(geo[g0 + 4], geo[g0 + 5])
    tangent = pair(geo[g0 + 6], geo[g0 + 7])
    for j in range(VPF):
        at = slice(8 * j, 8 * j + 8)
        cct[at, :] = trig_ref[0, at, :] * inv_cos
        tnt[at, :] = trig_ref[2, at, :] * tangent

    in_msg[b] = out_msg[b]
    for d in range(1, bands):
        msg_copy(b, lax.rem(b + d, bands)).wait_recv()

    got = jnp.concatenate(
        [
            pltpu.roll(jnp.concatenate([in_msg[h + d] for d in range(8)], axis=0), h * cols, 1, stride=cols, stride_axis=0)
            for h in range(0, bands, 8)
        ],
        axis=0,
    )
    own = lax.broadcasted_iota(jnp.int32, (bands, LANES), 1) // cols == lax.broadcasted_iota(jnp.int32, (bands, LANES), 0)

    def field(q, f):
        moved = pltpu.roll(got, (LANES - 32 * q - 8 * f) % LANES, 1)
        return jnp.sum(jnp.where(own, moved, 0.0), axis=0, keepdims=True)

    w0 = pair(field(0, 0), field(1, 0))
    w1 = pair(field(0, 1), field(1, 1))
    u = pair(field(0, 2), field(1, 2))
    v0, v1, vs, vn = field(0, 3), field(1, 3), field(2, 3), field(3, 3)
    @pl.when(first_col)
    def _():
        far_copy(0).wait_recv()

    wm = jnp.broadcast_to(in_msg[bands - 1], (8, LANES))
    fm = jnp.broadcast_to(far_edge[...], (8, LANES))
    em = jnp.broadcast_to(in_msg[0], (8, LANES))
    u_w = jnp.where(
        jnp.zeros_like(lane) + s == 0,
        pair(pltpu.roll(fm, LANES - 1 - (16 + cols - 1), 1), pltpu.roll(fm, LANES - 1 - (48 + cols - 1), 1)),
        pair(pltpu.roll(wm, LANES - 1 - 64, 1), pltpu.roll(wm, LANES - 1 - 65, 1)),
    )
    u_e = pair(pltpu.roll(em, LANES - 64, 1), pltpu.roll(em, LANES - 65, 1))
    c_west = 0.5 * (u + pltpu.roll(jnp.where(lane == LANES - 1, u_w, u), 1, 1))
    c_east = 0.5 * (u + pltpu.roll(jnp.where(lane == 0, u_e, u), LANES - 1, 1))
    c_south = 0.5 * pair(vs + v0, v0 + v1)
    c_north = 0.5 * pair(v0 + v1, v1 + vn)
    for j in range(VPF):
        at = slice(8 * j, 8 * j + 8)
        wnd[at, :] = w0 * trig_ref[0, at, :] + w1 * trig_ref[1, at, :]

    pack_copy(True).wait_recv()
    pack_copy(False).wait_recv()

    @pl.when(has_s)
    def _():
        mask_copy(True).wait_recv()

    @pl.when(has_n)
    def _():
        mask_copy(False).wait_recv()

    ms, mn = mask_s[...].astype(jnp.float32), mask_n[...].astype(jnp.float32)
    sea_s = pair(ms[0:1], ms[1:2])
    sea_n = pair(mn[0:1], mn[1:2])
    for i in range(GROUPS // 2):
        at = slice(8 * i, 8 * i + 8)
        pw, pe = pack_w[at, :], pack_e[at, :]
        pack[16 * i : 16 * i + 8, :] = jnp.where(low_half, pw, pltpu.roll(pe, 2, 1))
        pack[16 * i + 8 : 16 * i + 16, :] = jnp.where(low_half, pltpu.roll(pw, LANES - 2, 1), pe)

    def group(g, total):
        for i, first in enumerate(firsts):

            @pl.when((g == first) & has_s)
            def _(i=i):
                to_north(i).wait_recv()

            @pl.when((g == first) & has_n)
            def _(i=i):
                to_south(i).wait_recv()

        prow = pl.ds(pl.multiple_of(g * 8, 8), 8)
        beside = pack[prow, :]
        for k in range(FPG):
            f = g * FPG + k
            speed, growth, weight = wave[3 * f], wave[3 * f + 1], wave[3 * f + 2]
            base = g * GROUP_ROWS + k * ND * ROWS
            for j in range(VPF):
                at = slice(8 * j, 8 * j + 8)
                rows = pl.ds(pl.multiple_of(base + 8 * j, 8), 8)
                x = xv[rows, :] * sea_t
                halo = pltpu.roll(beside, LANES - (4 * (k * VPF + j) + 2), 1)
                w1, w2 = jnp.where(lane == LANES - 1, halo, x), jnp.where(lane >= LANES - 2, halo, x)
                e1, e2 = jnp.where(lane == 0, halo, x), jnp.where(lane < 2, halo, x)
                c = speed * cct[at, :]
                fw, fe = two_faces(
                    c + c_west, c + c_east,
                    pltpu.roll(w2, 2, 1), pltpu.roll(w1, 1, 1), x, pltpu.roll(e1, LANES - 1, 1), pltpu.roll(e2, LANES - 2, 1),
                )
                xs = south[rows, :] * sea_s
                xn = north[rows, :] * sea_n
                below = pair(pltpu.roll(xs, 7, 0), pltpu.roll(x, 1, 0))
                above = pair(pltpu.roll(x, 7, 0), pltpu.roll(xn, 1, 0))
                c = speed * trig_ref[1, at, :]
                fs, fn = two_faces(c + c_south, c + c_north, xs, below, x, above, xn)
                out = x - 0.5 * (fe - fw) - (metric_b * fn - metric_a * fs)
                pbuf[k, 8 + 8 * j : 16 + 8 * j, :] = out
                if j == 0:
                    pbuf[k, 8 + ND * ROWS : 16 + ND * ROWS, :] = out
                if j == VPF - 1:
                    pbuf[k, 0:8, :] = out
            for j in range(VPF):
                at = slice(8 * j, 8 * j + 8)
                o = 8 + 8 * j
                low2, low, mid, high = (pbuf[k, o + i : o + i + 8, :] for i in (-4, -2, 0, 2))
                d0, d1, d2 = low - low2, mid - low, high - mid
                flux = face(speed * tnt[at, :], low, mid, d1, d1 - d0, d2 - d1)
                fbuf[k, at, :] = flux
                if j == 0:
                    fbuf[k, ND * ROWS : ND * ROWS + 8, :] = flux
            square_sum = jnp.zeros((8, LANES), jnp.float32)
            for j in range(VPF):
                at = slice(8 * j, 8 * j + 8)
                rows = pl.ds(pl.multiple_of(base + 8 * j, 8), 8)
                turned = pbuf[k, 8 + 8 * j : 16 + 8 * j, :] - 0.5 * (fbuf[k, 8 * j + 2 : 8 * j + 10, :] - fbuf[k, at, :])
                square_sum = square_sum + turned * turned
                av[rows, :] = (sea_t * turned) * jnp.maximum(growth * wnd[at, :] + (1.0 - GROWTH), 1.0)
            total = total + weight * square_sum
        return total

    total = lax.fori_loop(0, GROUPS, group, jnp.zeros((8, LANES), jnp.float32))
    total = total + pltpu.roll(total, 4, 0)
    total = (total + pltpu.roll(total, 2, 0)) * (2.0 / (NF * ND))
    for f in range(NF):
        damp_ref[f] = 1.0 / (1.0 + total * ((f + 1.0) / NF))

    for i in range(len(PARTS)):

        @pl.when(has_n)
        def _(i=i):
            to_north(i).wait_send()

        @pl.when(has_s)
        def _(i=i):
            to_south(i).wait_send()

    for d in range(1, bands):
        msg_copy(lax.rem(b + d, bands), b).wait_send()

    @pl.when((b == 0) | passes_east)
    def _():
        edge_to_east.wait_send()

    @pl.when(far_corner)
    def _():
        for t in range(bands):
            far_copy(t).wait_send()

    pack_copy(True).wait_send()
    pack_copy(False).wait_send()

    @pl.when(has_n)
    def _():
        mask_copy(True).wait_send()

    @pl.when(has_s)
    def _():
        mask_copy(False).wait_send()


def damped(a_ref, damp_ref, o_hbm, ov, sem):
    for g in range(GROUPS):
        at = pl.ds(g * GROUP_ROWS, GROUP_ROWS)
        for k in range(FPG):
            factor = damp_ref[g * FPG + k]
            for j in range(VPF):
                rows = slice(g * GROUP_ROWS + 8 * (k * VPF + j), g * GROUP_ROWS + 8 * (k * VPF + j) + 8)
                ov[rows, :] = a_ref[rows, :] * factor
        pltpu.make_async_copy(ov.at[at], o_hbm.at[at], sem.at[g]).start()
    for g in range(GROUPS):
        at = pl.ds(g * GROUP_ROWS, GROUP_ROWS)
        pltpu.make_async_copy(ov.at[at], o_hbm.at[at], sem.at[g]).wait()


def per_device(bands, specs, spectra, sea_mask, wind, current):
    rows_all = ROWS_ALL
    geo, wave, trig = tables(bands)
    f32 = jnp.float32
    vmem = pl.BlockSpec(memory_space=pltpu.VMEM)
    hbm = pl.BlockSpec(memory_space=pl.ANY)
    dma = pltpu.SemaphoreType.DMA
    token = pltpu.SemaphoreType.REGULAR
    grown, damp = pl.pallas_call(
        functools.partial(kernel, bands, specs),
        out_shape=(
            pltpu.VMEM((rows_all, LANES), f32),
            pltpu.VMEM((NF, 8, LANES), f32),
        ),
        in_specs=[hbm] * 7,
        out_specs=(vmem, vmem),
        scratch_shapes=[
            pltpu.SMEM(geo.shape, f32),
            pltpu.SMEM(wave.shape, f32),
            pltpu.VMEM((ROWS, LANES), jnp.int32),
            pltpu.VMEM((2, LANES // bands, bands * ROWS), f32),
            pltpu.VMEM((2, LANES // bands, bands * ROWS), f32),
            pltpu.VMEM(trig.shape, f32),
            dma((6,)),
            pltpu.VMEM((rows_all, LANES), f32),
            pltpu.VMEM((rows_all, LANES), f32),
            pltpu.VMEM((rows_all, LANES), f32),
            pltpu.VMEM((ROWS, LANES), jnp.int32),
            pltpu.VMEM((ROWS, LANES), jnp.int32),
            pltpu.VMEM((LANES, LANES), f32),
            pltpu.VMEM((48, LANES), f32),
            pltpu.VMEM((bands, 1, LANES), f32),
            pltpu.VMEM((bands, 1, LANES), f32),
            pltpu.VMEM((bands, 1, LANES), f32),
            pltpu.VMEM((bands, 1, LANES), f32),
            pltpu.VMEM((1, LANES), f32),
            pltpu.VMEM((GROUPS * 8, LANES), f32),
            pltpu.VMEM((GROUPS * 4, LANES), f32),
            pltpu.VMEM((GROUPS * 4, LANES), f32),
            pltpu.VMEM((GROUPS * 4, LANES), f32),
            pltpu.VMEM((GROUPS * 4, LANES), f32),
            pltpu.VMEM((ND * ROWS, LANES), f32),
            pltpu.VMEM((ND * ROWS, LANES), f32),
            pltpu.VMEM((ND * ROWS, LANES), f32),
            pltpu.VMEM((FPG, ND * ROWS + 16, LANES), f32),
            pltpu.VMEM((FPG, ND * ROWS + 8, LANES), f32),
            dma(()), dma((bands,)), dma((bands,)), dma((3,)), dma((bands,)), token((3,)), token((4,)),
            dma((2,)), dma((2,)), dma((2,)), dma((2,)),
            *(dma((len(PARTS),)) for _ in range(4)),
        ],
        compiler_params=pltpu.CompilerParams(collective_id=0, has_side_effects=True),
        name="wave_step",
    )(
        jnp.asarray(geo), jnp.asarray(wave),
        spectra.reshape(rows_all, LANES), sea_mask,
        wind.transpose(0, 2, 1), current.transpose(0, 2, 1), jnp.asarray(trig),
    )
    out = pl.pallas_call(
        damped,
        out_shape=jax.ShapeDtypeStruct((rows_all, LANES), f32),
        in_specs=[vmem, vmem],
        out_specs=hbm,
        scratch_shapes=[pltpu.VMEM((rows_all, LANES), f32), dma((GROUPS,))],
        name="damped",
    )(*(pltpu.with_memory_space_constraint(v, pltpu.VMEM) for v in (grown, damp)))
    return out.reshape(NF * ND, ROWS, LANES)


def solution(mesh):
    placed = (
        P(None, "band", "spec"),
        P("band", "spec"),
        P(None, None, ("spec", "band")),
        P(None, None, ("spec", "band")),
    )
    return jax.shard_map(
        functools.partial(per_device, mesh.shape["band"], mesh.shape["spec"]),
        mesh=mesh, in_specs=placed, out_specs=P(None, "band", "spec"), check_vma=False,
    )
```

```python
import functools
import math

import jax
import jax.numpy as jnp
import numpy as np
from jax import lax
from jax.experimental import pallas as pl
from jax.experimental.pallas import tpu as pltpu
from jax.sharding import PartitionSpec as P

NF = 36
ND = 36

LAT_SOUTH = 30.0
LAT_NORTH = 55.0
SPEED_TOP = 0.35
FREQ_STEP = 1.1
TURNING = 1.5
GROWTH = 0.05
WIND_COUPLING = 0.04

MESH = pl.DeviceIdType.MESH
LANES = 128
ROWS = 2
VPF = ND * ROWS // 8
FPG = 3
GROUPS = NF // FPG
GROUP_ROWS = FPG * ND * ROWS
ROWS_ALL = NF * ND * ROWS
PARTS = (15, 9, 6, 3, 2, 1)
FIRST_PART = 1


def tables(bands):
    total = bands * ROWS
    rad = math.pi / 180.0

    def lat(p):
        return (LAT_SOUTH + (LAT_NORTH - LAT_SOUTH) * p / total) * rad

    geo = np.zeros((bands, 8), np.float64)
    for b in range(bands):
        y = b * ROWS
        c0, c1 = math.cos(lat(y + 0.5)), math.cos(lat(y + 1.5))
        fs, fm, fn = math.cos(lat(y)), math.cos(lat(y + 1)), math.cos(lat(y + 2))
        geo[b] = [
            1.0 / c0, 1.0 / c1,
            0.5 * fs / c0, 0.5 * fm / c1,
            0.5 * fm / c0, 0.5 * fn / c1,
            math.tan(lat(y + 0.5)), math.tan(lat(y + 1.5)),
        ]
    f = np.arange(NF)
    speed = SPEED_TOP * FREQ_STEP ** (-f)
    wave = np.stack([speed, GROWTH * WIND_COUPLING * FREQ_STEP**f, (f + 1.0) / NF], 1)
    theta = 2.0 * math.pi * np.arange(ND) / ND
    cos, sin = np.cos(theta), np.sin(theta)
    turn = -TURNING * 0.5 * (np.roll(cos, 1) + cos)

    def spread(v):
        return np.broadcast_to(np.repeat(v, ROWS)[:, None], (ND * ROWS, LANES))

    trig = np.stack([spread(cos), spread(sin), spread(turn)]).astype(np.float32)
    return geo.astype(np.float32).reshape(-1), wave.astype(np.float32).reshape(-1), trig


def face(c, low, high, step, bend_low, bend_high):
    bend = jnp.where(c >= 0.0, bend_low, bend_high)
    return c * (((low + high) - c * step) + (c * c * (1.0 / 3.0) - 1.0 / 3.0) * bend)


def two_faces(c_low, c_high, low2, low, mid, high, high2):
    d0, d1, d2, d3 = low - low2, mid - low, high - mid, high2 - high
    k0, k1, k2 = d1 - d0, d2 - d1, d3 - d2
    return face(c_low, low, mid, d1, k0, k1), face(c_high, mid, high, d2, k1, k2)


def kernel(
    bands, specs,
    geo_hbm, wave_hbm, x_hbm, mask_hbm, wind_hbm, cur_hbm, trig_hbm,
    av, damp_ref,
    geo, wave, mask_ref, wind_ref, cur_ref, trig_ref, small_sem,
    xv, south, north, mask_s, mask_n, square, strip, out_raw, out_msg, in_msg, edge_in, far_edge,
    pack, go_east, go_west, pack_w, pack_e, cct, tnt, wnd, pbuf, fbuf,
    x_sem, msg_send, msg_recv, edge_sem, far_send, tokens, late, pack_send, pack_recv, mask_send, mask_recv,
    n_send, s_send, n_recv, s_recv,
):
    b = lax.axis_index("band")
    s = lax.axis_index("spec")
    west, east = lax.rem(s + specs - 1, specs), lax.rem(s + 1, specs)
    has_n, has_s = b < bands - 1, b > 0
    up_band, down_band = jnp.minimum(b + 1, bands - 1), jnp.maximum(b - 1, 0)
    cols = LANES // bands

    barrier = pltpu.get_barrier_semaphore()
    first_col, last_col = s == 0, s == specs - 1
    pl.semaphore_signal(barrier, inc=1, device_id=(b, west), device_id_type=MESH)

    @pl.when(jnp.logical_not(last_col))
    def _():
        pl.semaphore_signal(barrier, inc=1, device_id=(b, east), device_id_type=MESH)

    def say(sem, target):
        pl.semaphore_signal(sem, inc=1, device_id=(target, s), device_id_type=MESH)

    partners = [b + bit - 2 * bit * lax.rem(b // bit, 2) for bit in (1, 2, 4, 8)]
    has_bit = [lax.rem(b // bit, 2) == 1 for bit in (1, 2, 4, 8)]
    say(barrier, partners[0])
    for i in range(1, 4):

        @pl.when(jnp.logical_not(has_bit[i]))
        def _(i=i):
            say(barrier, partners[i])

    odd = lax.rem(b, 2) == 1

    @pl.when(odd & has_n)
    def _():
        say(barrier, up_band)

    @pl.when(jnp.logical_not(odd) & has_s)
    def _():
        say(barrier, down_band)

    @pl.when(first_col & (b < bands - 1))
    def _():
        pl.semaphore_signal(barrier, inc=1, device_id=(bands - 1, west), device_id_type=MESH)

    small = [
        pltpu.make_async_copy(a, v, small_sem.at[i])
        for i, (a, v) in enumerate((
            (wind_hbm, wind_ref), (cur_hbm, cur_ref), (mask_hbm, mask_ref),
            (geo_hbm, geo), (wave_hbm, wave), (trig_hbm, trig_ref),
        ))
    ]
    for copy in small[:3]:
        copy.start()
    load = pltpu.make_async_copy(x_hbm, xv, x_sem)
    load.start()
    for copy in small[3:]:
        copy.start()

    sub = lax.broadcasted_iota(jnp.int32, (8, LANES), 0)
    lane = lax.broadcasted_iota(jnp.int32, (8, LANES), 1)
    even = lax.rem(sub, 2) == 0

    def pair(a, c):
        return jnp.where(even, a, c)

    square[...] = jnp.zeros_like(square)
    for copy in small[:3]:
        copy.wait()
    for i in range(2):
        square[i * 8 : i * 8 + cols, 0 : bands * ROWS] = wind_ref[i]
        square[16 + i * 8 : 16 + i * 8 + cols, 0 : bands * ROWS] = cur_ref[i]
    strip[...] = jnp.zeros_like(strip)
    strip[8 : 8 + bands * ROWS, :] = square[...].T[0 : bands * ROWS, :]
    message = strip[pl.ds(8, bands, stride=2), :]
    for q, first in ((1, 9), (2, 7), (3, 10)):
        message = message + pltpu.roll(strip[pl.ds(first, bands, stride=2), :], 32 * q, 1)
    for d in range(bands):
        out_raw[d] = message[d : d + 1]
        out_msg[d] = message[d : d + 1]

    sea = mask_ref[...].astype(jnp.float32)
    sea_t = pair(sea[0:1], sea[1:2])

    load.wait()

    def pack_group(g, carry):
        acc = jnp.zeros((8, LANES), jnp.float32)
        for i in range(FPG * VPF):
            v = xv[pl.ds(pl.multiple_of(g * GROUP_ROWS + 8 * i, 8), 8), :] * sea_t
            acc = jnp.where((lane >= 4 * i) & (lane < 4 * i + 4), pltpu.roll(v, 4 * i + 2, 1), acc)
        pack[pl.ds(pl.multiple_of(g * 8, 8), 8), :] = acc
        return carry

    lax.fori_loop(0, GROUPS, pack_group, 0)

    low_half = lax.rem(lane, 4) < 2
    for i in range(GROUPS // 2):
        two = [pack[16 * i + 8 * r : 16 * i + 8 * r + 8, :] for r in range(2)]
        at = slice(8 * i, 8 * i + 8)
        go_east[at, :] = jnp.where(low_half, two[0], pltpu.roll(two[1], 2, 1))
        go_west[at, :] = jnp.where(low_half, pltpu.roll(two[0], LANES - 2, 1), two[1])

    at_end = (b == 0) | (b == bands - 1)

    far_corner = last_col & (b == bands - 1)
    greeted = 4 - jnp.where(at_end, 1, 0) - jnp.where(first_col, 1, 0) + jnp.where(far_corner, bands - 1, 0)
    for i in range(1, 4):
        greeted = greeted + jnp.where(has_bit[i], 1, 0)
    pl.semaphore_wait(barrier, greeted)
    for i in range(1, 4):

        @pl.when(has_bit[i])
        def _(i=i):
            say(late.at[i], partners[i])

    @pl.when(last_col)
    def _():
        pl.semaphore_signal(late.at[0], inc=1, device_id=(b, 0), device_id_type=MESH)

    edge_to_east = pltpu.make_async_remote_copy(
        src_ref=out_raw, dst_ref=edge_in, send_sem=edge_sem.at[0], recv_sem=edge_sem.at[1],
        device_id=(b, east), device_id_type=MESH,
    )
    edge_to_west = pltpu.make_async_remote_copy(
        src_ref=out_raw, dst_ref=edge_in, send_sem=edge_sem.at[0], recv_sem=edge_sem.at[1],
        device_id=(b, west), device_id_type=MESH,
    )

    def far_copy(t):
        return pltpu.make_async_remote_copy(
            src_ref=out_raw.at[t], dst_ref=far_edge, send_sem=far_send.at[t], recv_sem=edge_sem.at[2],
            device_id=(t, 0), device_id_type=MESH,
        )

    @pl.when(far_corner)
    def _():
        for t in range(bands):
            far_copy(t).start()

    passes_east = (b == bands - 1) & jnp.logical_not(last_col)

    @pl.when(passes_east)
    def _():
        edge_to_east.start()

    @pl.when(jnp.logical_not(first_col))
    def _():
        far_edge[...] = jnp.zeros_like(far_edge)

    @pl.when((b == 0) & jnp.logical_not(first_col))
    def _():
        edge_to_west.start()

    firsts = [sum(PARTS[:i]) for i in range(len(PARTS))]

    def part(i):
        return pl.ds(firsts[i] * ND * ROWS, PARTS[i] * ND * ROWS)

    def to_north(i):
        return pltpu.make_async_remote_copy(
            src_ref=x_hbm.at[part(i)], dst_ref=south.at[part(i)], send_sem=n_send.at[i], recv_sem=s_recv.at[i],
            device_id=(up_band, s), device_id_type=MESH,
        )

    def to_south(i):
        return pltpu.make_async_remote_copy(
            src_ref=x_hbm.at[part(i)], dst_ref=north.at[part(i)], send_sem=s_send.at[i], recv_sem=n_recv.at[i],
            device_id=(down_band, s), device_id_type=MESH,
        )

    def mask_copy(northward):
        return pltpu.make_async_remote_copy(
            src_ref=mask_ref, dst_ref=mask_s if northward else mask_n,
            send_sem=mask_send.at[0 if northward else 1], recv_sem=mask_recv.at[0 if northward else 1],
            device_id=(up_band if northward else down_band, s), device_id_type=MESH,
        )

    def pack_copy(to_east):
        return pltpu.make_async_remote_copy(
            src_ref=go_east if to_east else go_west, dst_ref=pack_w if to_east else pack_e,
            send_sem=pack_send.at[0 if to_east else 1], recv_sem=pack_recv.at[0 if to_east else 1],
            device_id=(b, east if to_east else west), device_id_type=MESH,
        )

    @pl.when(has_n)
    def _():
        mask_copy(True).start()

    @pl.when(has_s)
    def _():
        mask_copy(False).start()

    pack_copy(True).start()

    @pl.when(jnp.logical_not(first_col))
    def _():
        pack_copy(False).start()

    def send_parts(some):
        for i in some:

            @pl.when(has_n)
            def _(i=i):
                to_north(i).start()

            @pl.when(has_s)
            def _(i=i):
                to_south(i).start()

    send_parts(range(FIRST_PART))

    for i in range(1, 4):

        @pl.when(jnp.logical_not(has_bit[i]))
        def _(i=i):
            pl.semaphore_wait(late.at[i], 1)

    for i in range(3):
        say(tokens.at[i], partners[i])
        pl.semaphore_wait(tokens.at[i], 1)

    def msg_copy(target, source):
        return pltpu.make_async_remote_copy(
            src_ref=out_msg.at[target], dst_ref=in_msg.at[source],
            send_sem=msg_send.at[target], recv_sem=msg_recv.at[source],
            device_id=(target, s), device_id_type=MESH,
        )

    @pl.when((b == 0) | ((b == bands - 1) & jnp.logical_not(first_col)))
    def _():
        edge_to_east.wait_recv()
        edge = jnp.concatenate([edge_in[d] for d in range(bands)], axis=0)
        wide = lax.broadcasted_iota(jnp.int32, (bands, LANES), 1)
        last = (lax.broadcasted_iota(jnp.int32, (bands, LANES), 0) * 0 + b) > 0
        first_row = jnp.where(last, pltpu.roll(edge, 64 - (16 + cols - 1), 1), pltpu.roll(edge, 64 - 16, 1))
        second_row = jnp.where(last, pltpu.roll(edge, 65 - (48 + cols - 1), 1), pltpu.roll(edge, 65 - 48, 1))
        plain = jnp.concatenate([out_raw[d] for d in range(bands)], axis=0)
        merged = jnp.where(wide == 64, first_row, jnp.where(wide == 65, second_row, plain))
        for d in range(bands):
            out_msg[d] = merged[d : d + 1]

    for d in range(1, bands):
        msg_copy(lax.rem(b + d, bands), b).start()

    @pl.when(first_col)
    def _():
        pl.semaphore_wait(late.at[0], 1)

        @pl.when(b == 0)
        def _():
            edge_to_west.start()

        pack_copy(False).start()

    send_parts(range(FIRST_PART, len(PARTS)))

    @pl.when(b == 0)
    def _():
        mask_s[...] = jnp.zeros_like(mask_s)

        def clear(i, carry):
            south[pl.ds(pl.multiple_of(i * GROUP_ROWS, 8), GROUP_ROWS), :] = jnp.zeros((GROUP_ROWS, LANES), jnp.float32)
            return carry

        lax.fori_loop(0, GROUPS, clear, 0)

    @pl.when(b == bands - 1)
    def _():
        mask_n[...] = jnp.zeros_like(mask_n)

        def clear(i, carry):
            north[pl.ds(pl.multiple_of(i * GROUP_ROWS, 8), GROUP_ROWS), :] = jnp.zeros((GROUP_ROWS, LANES), jnp.float32)
            return carry

        lax.fori_loop(0, GROUPS, clear, 0)

    for copy in small[3:]:
        copy.wait()
    g0 = b * 8
    inv_cos = pair(geo[g0], geo[g0 + 1])
    metric_a = pair(geo[g0 + 2], geo[g0 + 3])
    metric_b = pair(geo[g0 + 4], geo[g0 + 5])
    tangent = pair(geo[g0 + 6], geo[g0 + 7])
    for j in range(VPF):
        at = slice(8 * j, 8 * j + 8)
        cct[at, :] = trig_ref[0, at, :] * inv_cos
        tnt[at, :] = trig_ref[2, at, :] * tangent

    in_msg[b] = out_msg[b]
    for d in range(1, bands):
        msg_copy(b, lax.rem(b + d, bands)).wait_recv()

    got = jnp.concatenate(
        [
            pltpu.roll(jnp.concatenate([in_msg[h + d] for d in range(8)], axis=0), h * cols, 1, stride=cols, stride_axis=0)
            for h in range(0, bands, 8)
        ],
        axis=0,
    )
    own = lax.broadcasted_iota(jnp.int32, (bands, LANES), 1) // cols == lax.broadcasted_iota(jnp.int32, (bands, LANES), 0)

    def field(q, f):
        moved = pltpu.roll(got, (LANES - 32 * q - 8 * f) % LANES, 1)
        return jnp.sum(jnp.where(own, moved, 0.0), axis=0, keepdims=True)

    w0 = pair(field(0, 0), field(1, 0))
    w1 = pair(field(0, 1), field(1, 1))
    u = pair(field(0, 2), field(1, 2))
    v0, v1, vs, vn = field(0, 3), field(1, 3), field(2, 3), field(3, 3)
    @pl.when(first_col)
    def _():
        far_copy(0).wait_recv()

    wm = jnp.broadcast_to(in_msg[bands - 1], (8, LANES))
    fm = jnp.broadcast_to(far_edge[...], (8, LANES))
    em = jnp.broadcast_to(in_msg[0], (8, LANES))
    u_w = jnp.where(
        jnp.zeros_like(lane) + s == 0,
        pair(pltpu.roll(fm, LANES - 1 - (16 + cols - 1), 1), pltpu.roll(fm, LANES - 1 - (48 + cols - 1), 1)),
        pair(pltpu.roll(wm, LANES - 1 - 64, 1), pltpu.roll(wm, LANES - 1 - 65, 1)),
    )
    u_e = pair(pltpu.roll(em, LANES - 64, 1), pltpu.roll(em, LANES - 65, 1))
    c_west = 0.5 * (u + pltpu.roll(jnp.where(lane == LANES - 1, u_w, u), 1, 1))
    c_east = 0.5 * (u + pltpu.roll(jnp.where(lane == 0, u_e, u), LANES - 1, 1))
    c_south = 0.5 * pair(vs + v0, v0 + v1)
    c_north = 0.5 * pair(v0 + v1, v1 + vn)
    for j in range(VPF):
        at = slice(8 * j, 8 * j + 8)
        wnd[at, :] = w0 * trig_ref[0, at, :] + w1 * trig_ref[1, at, :]

    pack_copy(True).wait_recv()
    pack_copy(False).wait_recv()

    @pl.when(has_s)
    def _():
        mask_copy(True).wait_recv()

    @pl.when(has_n)
    def _():
        mask_copy(False).wait_recv()

    ms, mn = mask_s[...].astype(jnp.float32), mask_n[...].astype(jnp.float32)
    sea_s = pair(ms[0:1], ms[1:2])
    sea_n = pair(mn[0:1], mn[1:2])
    for i in range(GROUPS // 2):
        at = slice(8 * i, 8 * i + 8)
        pw, pe = pack_w[at, :], pack_e[at, :]
        pack[16 * i : 16 * i + 8, :] = jnp.where(low_half, pw, pltpu.roll(pe, 2, 1))
        pack[16 * i + 8 : 16 * i + 16, :] = jnp.where(low_half, pltpu.roll(pw, LANES - 2, 1), pe)

    def arrived(f):
        for i, first in enumerate(firsts):

            @pl.when((f == first) & has_s)
            def _(i=i):
                to_north(i).wait_recv()

            @pl.when((f == first) & has_n)
            def _(i=i):
                to_south(i).wait_recv()

    def group(g, total, last=False):
        arrived(g * FPG)
        prow = pl.ds(pl.multiple_of(g * 8, 8), 8)
        beside = pack[prow, :]
        for k in range(FPG):
            f = g * FPG + k
            if last and k:
                arrived(f)
            speed, growth, weight = wave[3 * f], wave[3 * f + 1], wave[3 * f + 2]
            base = g * GROUP_ROWS + k * ND * ROWS
            for j in range(VPF):
                at = slice(8 * j, 8 * j + 8)
                rows = pl.ds(pl.multiple_of(base + 8 * j, 8), 8)
                x = xv[rows, :] * sea_t
                halo = pltpu.roll(beside, LANES - (4 * (k * VPF + j) + 2), 1)
                w1, w2 = jnp.where(lane == LANES - 1, halo, x), jnp.where(lane >= LANES - 2, halo, x)
                e1, e2 = jnp.where(lane == 0, halo, x), jnp.where(lane < 2, halo, x)
                c = speed * cct[at, :]
                fw, fe = two_faces(
                    c + c_west, c + c_east,
                    pltpu.roll(w2, 2, 1), pltpu.roll(w1, 1, 1), x, pltpu.roll(e1, LANES - 1, 1), pltpu.roll(e2, LANES - 2, 1),
                )
                xs = south[rows, :] * sea_s
                xn = north[rows, :] * sea_n
                below = pair(pltpu.roll(xs, 7, 0), pltpu.roll(x, 1, 0))
                above = pair(pltpu.roll(x, 7, 0), pltpu.roll(xn, 1, 0))
                c = speed * trig_ref[1, at, :]
                fs, fn = two_faces(c + c_south, c + c_north, xs, below, x, above, xn)
                out = x - 0.5 * (fe - fw) - (metric_b * fn - metric_a * fs)
                pbuf[k, 8 + 8 * j : 16 + 8 * j, :] = out
                if j == 0:
                    pbuf[k, 8 + ND * ROWS : 16 + ND * ROWS, :] = out
                if j == VPF - 1:
                    pbuf[k, 0:8, :] = out
            for j in range(VPF):
                at = slice(8 * j, 8 * j + 8)
                o = 8 + 8 * j
                low2, low, mid, high = (pbuf[k, o + i : o + i + 8, :] for i in (-4, -2, 0, 2))
                d0, d1, d2 = low - low2, mid - low, high - mid
                flux = face(speed * tnt[at, :], low, mid, d1, d1 - d0, d2 - d1)
                fbuf[k, at, :] = flux
                if j == 0:
                    fbuf[k, ND * ROWS : ND * ROWS + 8, :] = flux
            square_sum = jnp.zeros((8, LANES), jnp.float32)
            for j in range(VPF):
                at = slice(8 * j, 8 * j + 8)
                rows = pl.ds(pl.multiple_of(base + 8 * j, 8), 8)
                turned = pbuf[k, 8 + 8 * j : 16 + 8 * j, :] - 0.5 * (fbuf[k, 8 * j + 2 : 8 * j + 10, :] - fbuf[k, at, :])
                square_sum = square_sum + turned * turned
                av[rows, :] = (sea_t * turned) * jnp.maximum(growth * wnd[at, :] + (1.0 - GROWTH), 1.0)
            total = total + weight * square_sum
        return total

    total = lax.fori_loop(0, GROUPS - 1, group, jnp.zeros((8, LANES), jnp.float32))
    total = group(jnp.int32(GROUPS - 1), total, last=True)
    total = total + pltpu.roll(total, 4, 0)
    total = (total + pltpu.roll(total, 2, 0)) * (2.0 / (NF * ND))
    for f in range(NF):
        damp_ref[f] = 1.0 / (1.0 + total * ((f + 1.0) / NF))

    for i in range(len(PARTS)):

        @pl.when(has_n)
        def _(i=i):
            to_north(i).wait_send()

        @pl.when(has_s)
        def _(i=i):
            to_south(i).wait_send()

    for d in range(1, bands):
        msg_copy(lax.rem(b + d, bands), b).wait_send()

    @pl.when((b == 0) | passes_east)
    def _():
        edge_to_east.wait_send()

    @pl.when(far_corner)
    def _():
        for t in range(bands):
            far_copy(t).wait_send()

    pack_copy(True).wait_send()
    pack_copy(False).wait_send()

    @pl.when(has_n)
    def _():
        mask_copy(True).wait_send()

    @pl.when(has_s)
    def _():
        mask_copy(False).wait_send()


def damped(a_ref, damp_ref, o_hbm, ov, sem):
    for g in range(GROUPS):
        at = pl.ds(g * GROUP_ROWS, GROUP_ROWS)
        for k in range(FPG):
            factor = damp_ref[g * FPG + k]
            for j in range(VPF):
                rows = slice(g * GROUP_ROWS + 8 * (k * VPF + j), g * GROUP_ROWS + 8 * (k * VPF + j) + 8)
                ov[rows, :] = a_ref[rows, :] * factor
        pltpu.make_async_copy(ov.at[at], o_hbm.at[at], sem.at[g]).start()
    for g in range(GROUPS):
        at = pl.ds(g * GROUP_ROWS, GROUP_ROWS)
        pltpu.make_async_copy(ov.at[at], o_hbm.at[at], sem.at[g]).wait()


def per_device(bands, specs, spectra, sea_mask, wind, current):
    rows_all = ROWS_ALL
    geo, wave, trig = tables(bands)
    f32 = jnp.float32
    vmem = pl.BlockSpec(memory_space=pltpu.VMEM)
    hbm = pl.BlockSpec(memory_space=pl.ANY)
    dma = pltpu.SemaphoreType.DMA
    token = pltpu.SemaphoreType.REGULAR
    grown, damp = pl.pallas_call(
        functools.partial(kernel, bands, specs),
        out_shape=(
            pltpu.VMEM((rows_all, LANES), f32),
            pltpu.VMEM((NF, 8, LANES), f32),
        ),
        in_specs=[hbm] * 7,
        out_specs=(vmem, vmem),
        scratch_shapes=[
            pltpu.SMEM(geo.shape, f32),
            pltpu.SMEM(wave.shape, f32),
            pltpu.VMEM((ROWS, LANES), jnp.int32),
            pltpu.VMEM((2, LANES // bands, bands * ROWS), f32),
            pltpu.VMEM((2, LANES // bands, bands * ROWS), f32),
            pltpu.VMEM(trig.shape, f32),
            dma((6,)),
            pltpu.VMEM((rows_all, LANES), f32),
            pltpu.VMEM((rows_all, LANES), f32),
            pltpu.VMEM((rows_all, LANES), f32),
            pltpu.VMEM((ROWS, LANES), jnp.int32),
            pltpu.VMEM((ROWS, LANES), jnp.int32),
            pltpu.VMEM((LANES, LANES), f32),
            pltpu.VMEM((48, LANES), f32),
            pltpu.VMEM((bands, 1, LANES), f32),
            pltpu.VMEM((bands, 1, LANES), f32),
            pltpu.VMEM((bands, 1, LANES), f32),
            pltpu.VMEM((bands, 1, LANES), f32),
            pltpu.VMEM((1, LANES), f32),
            pltpu.VMEM((GROUPS * 8, LANES), f32),
            pltpu.VMEM((GROUPS * 4, LANES), f32),
            pltpu.VMEM((GROUPS * 4, LANES), f32),
            pltpu.VMEM((GROUPS * 4, LANES), f32),
            pltpu.VMEM((GROUPS * 4, LANES), f32),
            pltpu.VMEM((ND * ROWS, LANES), f32),
            pltpu.VMEM((ND * ROWS, LANES), f32),
            pltpu.VMEM((ND * ROWS, LANES), f32),
            pltpu.VMEM((FPG, ND * ROWS + 16, LANES), f32),
            pltpu.VMEM((FPG, ND * ROWS + 8, LANES), f32),
            dma(()), dma((bands,)), dma((bands,)), dma((3,)), dma((bands,)), token((3,)), token((4,)),
            dma((2,)), dma((2,)), dma((2,)), dma((2,)),
            *(dma((len(PARTS),)) for _ in range(4)),
        ],
        compiler_params=pltpu.CompilerParams(collective_id=0, has_side_effects=True),
        name="wave_step",
    )(
        jnp.asarray(geo), jnp.asarray(wave),
        spectra.reshape(rows_all, LANES), sea_mask,
        wind.transpose(0, 2, 1), current.transpose(0, 2, 1), jnp.asarray(trig),
    )
    out = pl.pallas_call(
        damped,
        out_shape=jax.ShapeDtypeStruct((rows_all, LANES), f32),
        in_specs=[vmem, vmem],
        out_specs=hbm,
        scratch_shapes=[pltpu.VMEM((rows_all, LANES), f32), dma((GROUPS,))],
        name="damped",
    )(*(pltpu.with_memory_space_constraint(v, pltpu.VMEM) for v in (grown, damp)))
    return out.reshape(NF * ND, ROWS, LANES)


def solution(mesh):
    placed = (
        P(None, "band", "spec"),
        P("band", "spec"),
        P(None, None, ("spec", "band")),
        P(None, None, ("spec", "band")),
    )
    return jax.shard_map(
        functools.partial(per_device, mesh.shape["band"], mesh.shape["spec"]),
        mesh=mesh, in_specs=placed, out_specs=P(None, "band", "spec"), check_vma=False,
    )
```
